512 devices in a mesh: seq: 64 (over z, x), head: 8 (over y, core).
Axes of the slice: x: 4, y: 4, z: 16, core: 2. Of those that a mesh axis runs over, the one named last changes fastest.
Arguments:
- query_one: bfloat16 [8192, 32, 128], P('seq', 'head'), may hold values from -6 to 6
- key_one: bfloat16 [8192, 32, 128], P('seq', 'head'), may hold values from -6 to 6
- value_one: bfloat16 [8192, 32, 128], P('seq', 'head'), may hold values from -160 to 160
- log_decay: float32 [32, 8192], P('head', 'seq'), may hold values from -1 to 0
- query_two: bfloat16 [8192, 32, 128], P('seq', 'head'), may hold values from -24 to 24
- key_two: bfloat16 [8192, 32, 128], P('seq', 'head'), may hold values from -24 to 24
- out_grad: bfloat16 [8192, 32, 128], P('seq', 'head'), may hold values from -6 to 6
- doc_ids: int32 [64], replicated, may hold values from 0 to 15, never falling along the last dimension, each value on 1 to 8 neighbouring positions
Outputs:
- grad_query_one: float32 [8192, 32, 128], P('seq', 'head')
- grad_key_one: float32 [8192, 32, 128], P('seq', 'head')
- grad_value_one: float32 [8192, 32, 128], P('seq', 'head')
- grad_query_two: float32 [8192, 32, 128], P('seq', 'head')
- grad_key_two: float32 [8192, 32, 128], P('seq', 'head')
The draws below stay inside these ranges and needn't reach their ends.
Inputs may be any that keep to these rules, and one draw needn't show every extreme that they name: doc_ids never fall along the sequence; one document covers at most 8 blocks.
All inputs are finite; a program needn't handle non-finite values.
Results may differ from the reference program's by a relative error of at most 0.0096.
Values may be sent and summed in bfloat16 or wider, within the bound.
A program may use at most 128 MiB of HBM per device.

```python
import math
import jax
import jax.numpy as jnp
import numpy as np
from jax import lax

HEADS = 32
HEAD_DIM = 128
BLOCK = 128
BLK_DEV = 1
REACH = 8
SEQUENCE_LENGTH = 8192
NBLK = 64
DOC_BLOCKS = 8
DOCS = 16


def draw_query_two(key, part):
    noise_key = jax.random.fold_in(key, 11)
    field = jnp.clip(jax.random.normal(noise_key, (SEQUENCE_LENGTH, HEADS, HEAD_DIM), jnp.float32), -6.0, 6.0)
    return field.astype(jnp.bfloat16)


def draw_key_two(key, part):
    noise_key = jax.random.fold_in(key, 13)
    field = jnp.clip(jax.random.normal(noise_key, (SEQUENCE_LENGTH, HEADS, HEAD_DIM), jnp.float32), -6.0, 6.0)
    return field.astype(jnp.bfloat16)


def draw_value_one(key, part):
    noise_key, row_key, column_key = jax.random.split(jax.random.fold_in(key, 21), 3)
    heads_share = jnp.arange(HEADS, dtype=jnp.float32) / max(HEADS - 1, 1)
    noise = jnp.clip(jax.random.normal(noise_key, (SEQUENCE_LENGTH, HEADS, HEAD_DIM), jnp.float32), -4.0, 4.0)
    rising = 3.0 ** heads_share
    row_scale = jnp.exp(jax.random.uniform(row_key, (SEQUENCE_LENGTH, 1, 1), jnp.float32, -1.15, 1.15))
    column_scale = jnp.exp(jax.random.uniform(column_key, (1, HEADS, HEAD_DIM), jnp.float32, -1.15, 1.15))
    return (noise * row_scale * column_scale * rising[None, :, None]).astype(jnp.bfloat16)


def draw_log_decay(key, part):
    every_key = jax.random.split(jax.random.fold_in(key, 31), 7)
    order = jax.random.permutation(every_key[0], HEADS)
    fast_count = HEADS // 2
    fast_heads = order < fast_count
    fast_rate = jnp.exp(jax.random.uniform(every_key[1], (HEADS,), jnp.float32, math.log(1.0 / 50.0), math.log(1.0 / 30.0)))
    slow_rate = jnp.exp(jax.random.uniform(every_key[2], (HEADS,), jnp.float32, math.log(0.05), math.log(0.3))) * (math.log(10.0) / SEQUENCE_LENGTH)
    rate = jnp.where(fast_heads, fast_rate, slow_rate)
    block_factor = jnp.exp(jax.random.uniform(every_key[3], (HEADS, NBLK), jnp.float32, -0.7, 0.7))
    roughness = jnp.exp(jax.random.uniform(every_key[4], (HEADS, SEQUENCE_LENGTH), jnp.float32, -0.35, 0.35))
    position_values = rate[:, None] * jnp.repeat(block_factor, BLOCK, axis=1) * roughness
    segment_start = jax.random.randint(every_key[5], (2,), 0, SEQUENCE_LENGTH)
    segment_length = jax.random.uniform(every_key[6], (2,), jnp.float32, math.log(0.5), math.log(0.8))
    token_position = jnp.arange(SEQUENCE_LENGTH)
    segment_list = jnp.where(token_position == segment_start[0], segment_length[0], 0.0) + jnp.where(token_position == segment_start[1], segment_length[1], 0.0)
    return (segment_list[None, :] - position_values).astype(jnp.float32)


def block_levels(rng, dims, cuts, smallest, largest):
    def one(position, parts):
        draws = jax.random.uniform(jax.random.fold_in(jax.random.fold_in(rng, 6), position), (parts,), jnp.float32, smallest / len(cuts), largest / len(cuts))
        return jnp.repeat(jnp.exp(draws), dims[position] // parts).reshape((-1,) + (1,) * (len(dims) - position - 1))

    level = one(*cuts[0])
    for cut in cuts[1:]:
        level = level * one(*cut)
    return level


def length_profile(count, total, bound, lean):
    weights = [(1 << 20) // math.isqrt(standing ** lean) + 1 for standing in range(2, count + 1)]
    spare, holding = total - bound - (count - 1), [1] * (count - 1)
    while spare > 0:
        free = [i for i in range(count - 1) if holding[i] < bound]
        whole, left = sum([weights[i] for i in free]), spare
        for i in free:
            more = min(bound - holding[i], max(1, left * weights[i] // whole), spare)
            holding[i] = holding[i] + more
            spare = spare - more
    return np.array([bound] + holding)


def uneven(stream_key, number_of, total, reach, skew):
    if number_of == 2:
        one = jax.random.randint(stream_key, (), max(1, total - reach), min(reach, total - 1) + 1)
        return jnp.stack([one, total - one])
    lengths = jnp.asarray(length_profile(number_of, total, reach, skew), jnp.int32)
    twos = (number_of - 1) // 2
    donor, taker = lengths[1:1 + 2 * twos:2], lengths[2:2 + 2 * twos:2]
    room = jnp.minimum(donor - 1, reach - taker)
    passed = jax.random.randint(jax.random.fold_in(stream_key, 1), (twos,), 0, 1 << 20) % (room + 1)
    lengths = lengths.at[1:1 + 2 * twos:2].set(donor - passed).at[2:2 + 2 * twos:2].set(taker + passed)
    return lengths[jax.random.permutation(jax.random.fold_in(stream_key, 2), number_of)]


def centred(key, dims, width, most, cuts=(), kind=jnp.bfloat16):
    result = width * jax.random.normal(key, dims, jnp.float32)
    if cuts:
        result = result * block_levels(key, dims, cuts, -0.22, 0.18)
    return jnp.clip(result, -most, most).astype(kind)


def setup_inputs(seed: int = 0) -> dict:
    key_of = jax.random.split(jax.random.key(seed), 9)
    query_one = centred(key_of[0], (SEQUENCE_LENGTH, HEADS, HEAD_DIM), 1.0, 6.0, ((0, 64), (1, 8)))
    key_one = centred(key_of[1], (SEQUENCE_LENGTH, HEADS, HEAD_DIM), 1.0, 6.0, ((0, 64), (1, 8)))
    value_one = draw_value_one(jax.random.fold_in(key_of[8], 71), 0)
    log_decay = draw_log_decay(jax.random.fold_in(key_of[8], 71), 0)
    query_two = draw_query_two(jax.random.fold_in(key_of[8], 71), 0)
    key_two = draw_key_two(jax.random.fold_in(key_of[8], 71), 0)
    out_grad = centred(key_of[6], (SEQUENCE_LENGTH, HEADS, HEAD_DIM), 1.0, 6.0, ((0, 64), (1, 8)))
    doc_ids = jnp.searchsorted(jnp.cumsum(uneven(key_of[7], DOCS, NBLK, DOC_BLOCKS, 1)), jnp.arange(NBLK), side="right").astype(jnp.int32)
    return dict(query_one=query_one, key_one=key_one, value_one=value_one, log_decay=log_decay, query_two=query_two, key_two=key_two, out_grad=out_grad, doc_ids=doc_ids)


exact_precision = lax.Precision.HIGHEST
floor_score = -1e+30
norm_epsilon = 1e-05

def lower_mask(length):
    return lax.broadcasted_iota(jnp.int32, (length, length), 0) >= lax.broadcasted_iota(jnp.int32, (length, length), 1)

def shard_output(q_float, k_float, v_float, cumulative, incoming):
    lower = lower_mask(q_float.shape[0])[None]
    gaps = cumulative[:, :, None] - cumulative[:, None, :]
    weights = jnp.where(lower, jnp.exp(jnp.where(lower, gaps, 0.0)), 0.0)
    scores = jnp.einsum('thd,uhd->htu', q_float, k_float, precision=exact_precision) * weights
    inner_part = jnp.einsum('htu,uhe->the', scores, v_float, precision=exact_precision)
    outer_part = jnp.einsum('thd,hde->the', q_float * jnp.exp(cumulative).T[:, :, None], incoming, precision=exact_precision)
    return inner_part + outer_part

def shard_state(k_float, v_float, cumulative):
    tail_decay = jnp.exp(cumulative[:, -1:] - cumulative)
    return jnp.einsum('uhd,uhe->hde', k_float * tail_decay.T[:, :, None], v_float, precision=exact_precision)

def linear_layer(q_float, k_float, v_float, log_decay):
    length = BLK_DEV * BLOCK
    shards = SEQUENCE_LENGTH // length

    def split_rows(values):
        return values.reshape(shards, length, HEADS, HEAD_DIM)
    decays = log_decay.reshape(HEADS, shards, length).transpose(1, 0, 2)

    def advance(state_now, pieces):
        query_rows, key_rows, value_rows, decay_rows = pieces
        cumulative = jnp.cumsum(decay_rows, axis=1)
        output_rows = shard_output(query_rows, key_rows, value_rows, cumulative, state_now)
        state_next = jnp.exp(cumulative[:, -1])[:, None, None] * state_now + shard_state(key_rows, value_rows, cumulative)
        return (state_next, output_rows)
    start_state = jnp.zeros((HEADS, HEAD_DIM, HEAD_DIM), q_float.dtype)
    final_state, outputs = lax.scan(advance, start_state, (split_rows(q_float), split_rows(k_float), split_rows(v_float), decays))
    raw_out = outputs.reshape(SEQUENCE_LENGTH, HEADS, HEAD_DIM)
    mean_square = lax.optimization_barrier(jnp.mean(raw_out * raw_out, axis=(1, 2), keepdims=True))
    return raw_out / jnp.sqrt(mean_square + norm_epsilon)

def rounded(values):
    return lax.optimization_barrier(values.astype(jnp.bfloat16)).astype(jnp.float32)

def softmax_layer(query_two, key_two, values_two, out_grad, doc_ids):
    length = BLK_DEV * BLOCK
    shards = SEQUENCE_LENGTH // length
    window = (REACH + 1) * length
    margin = REACH * length
    scale = 1.0 / math.sqrt(HEAD_DIM)
    token_doc = jnp.repeat(doc_ids.astype(jnp.int32), BLOCK)
    q_float = query_two.astype(jnp.float32)
    grad_float = out_grad.astype(jnp.float32)
    padding = jnp.zeros((margin, HEADS, HEAD_DIM), jnp.float32)
    k_padded = jnp.concatenate([padding, key_two.astype(jnp.float32)], axis=0)
    v_padded = jnp.concatenate([padding, values_two.astype(jnp.float32)], axis=0)
    doc_padded = jnp.concatenate([jnp.full((margin,), -1, jnp.int32), token_doc])
    pos_padded = jnp.arange(SEQUENCE_LENGTH + margin, dtype=jnp.int32) - margin

    def visit(totals, shard):
        key_total, value_total = totals
        start = (shard * length).astype(jnp.int32)
        query_rows = lax.dynamic_slice_in_dim(q_float, start, length, 0)
        grad_rows = lax.dynamic_slice_in_dim(grad_float, start, length, 0)
        query_doc = lax.dynamic_slice_in_dim(token_doc, start, length, 0)
        query_pos = start + jnp.arange(length, dtype=jnp.int32)
        key_rows = lax.dynamic_slice_in_dim(k_padded, start, window, 0)
        value_rows = lax.dynamic_slice_in_dim(v_padded, start, window, 0)
        key_doc = lax.dynamic_slice_in_dim(doc_padded, start, window, 0)
        key_pos = lax.dynamic_slice_in_dim(pos_padded, start, window, 0)
        allowed = (key_pos[None, :] <= query_pos[:, None]) & (key_pos[None, :] >= 0) & (key_doc[None, :] == query_doc[:, None])
        scores = jnp.einsum('thd,uhd->htu', query_rows, key_rows) * scale
        scores = jnp.where(allowed[None], scores, floor_score)
        peak = lax.optimization_barrier(jnp.max(scores, axis=2, keepdims=True))
        mass = lax.optimization_barrier(jnp.sum(jnp.where(allowed[None], jnp.exp(scores - peak), 0.0), axis=2, keepdims=True))
        log_mass = peak + jnp.log(mass)
        prob = jnp.where(allowed[None], jnp.exp(scores - log_mass), 0.0)
        prob_low = rounded(prob)
        attended = jnp.einsum('htu,uhd->thd', prob_low, value_rows)
        delta = lax.optimization_barrier(jnp.sum(grad_rows * attended, axis=2))
        grad_prob = jnp.einsum('thd,uhd->htu', grad_rows, value_rows)
        grad_score = rounded(prob * (grad_prob - delta.T[:, :, None]) * scale)
        query_grad = jnp.einsum('htu,uhd->thd', grad_score, key_rows)
        key_grad = jnp.einsum('htu,thd->uhd', grad_score, query_rows)
        value_grad = jnp.einsum('htu,thd->uhd', prob_low, grad_rows)
        key_total = lax.dynamic_update_slice_in_dim(key_total, lax.dynamic_slice_in_dim(key_total, start, window, 0) + key_grad, start, 0)
        value_total = lax.dynamic_update_slice_in_dim(value_total, lax.dynamic_slice_in_dim(value_total, start, window, 0) + value_grad, start, 0)
        return ((key_total, value_total), query_grad)
    zero_total = jnp.zeros((SEQUENCE_LENGTH + margin, HEADS, HEAD_DIM), jnp.float32)
    totals, query_grads = lax.scan(visit, (zero_total, zero_total), jnp.arange(shards, dtype=jnp.int32))
    grad_query_two = query_grads.reshape(SEQUENCE_LENGTH, HEADS, HEAD_DIM)
    return (grad_query_two, totals[0][margin:], totals[1][margin:])

def reference(query_one, key_one, value_one, log_decay, query_two, key_two, out_grad, doc_ids):

    def forward_one(q_float, k_float, v_float):
        return linear_layer(q_float, k_float, v_float, log_decay)
    normed, pull_back = jax.vjp(forward_one, query_one.astype(jnp.float32), key_one.astype(jnp.float32), value_one.astype(jnp.float32))
    values_two = normed.astype(jnp.bfloat16)
    grad_query_two, grad_key_two, grad_values_two = softmax_layer(query_two, key_two, values_two, out_grad, doc_ids)
    grad_query_one, grad_key_one, grad_value_one = pull_back(grad_values_two)
    return (grad_query_one, grad_key_one, grad_value_one, grad_query_two, grad_key_two)
```

```python
import functools
import math

import jax
import jax.numpy as jnp
from jax import lax
from jax.experimental import pallas as pl
from jax.experimental.pallas import tpu as pltpu
from jax.sharding import PartitionSpec as P

BLOCK = 128
ROW = 4
NORM_EPSILON = 1e-05
FLOOR = -1e30
MESH = pl.DeviceIdType.MESH
F32 = jnp.float32
BF16 = jnp.bfloat16

(LD, K1, V1, K2, Q2, GO, Q1, SC1, DEC, SC2, KA, KB, QA, QB, GA, GB, LA, LB, PLN,
 SC3, SC4, VA, VB, DA, DB, O0, O1, O2, O3, O4) = range(30)
NSEM = 30

NN = (((1,), (0,)), ((), ()))
NT = (((1,), (1,)), ((), ()))
TN = (((0,), (0,)), ((), ()))


def dot(a, b, dims):
    return lax.dot_general(a, b, dims, preferred_element_type=F32)


def split(a):
    high = a.astype(BF16)
    return high, (a - high.astype(F32)).astype(BF16)


def dot_l(a, b, dims):
    high, low = split(a)
    return dot(high, b, dims) + dot(low, b, dims)


def dot_r(a, b, dims):
    high, low = split(b)
    return dot(a, high, dims) + dot(a, low, dims)


def kernel(Z, X, H, width_all, q1, k1, v1, q2, k2, go, ld, docs,
           o_q1, o_k1, o_v1, o_q2, o_k2,
           q1b, k1b, v1b, kall, qall, gall, vall, ldb, gcol, grow,
           wts, aw, pf, pt, lser, delr, lsall, dlall,
           sst, sbuf, mst, mbuf, sst2, sbuf2, mst2, mbuf2, abuf, arow,
           raw, gv, rr, pls, plb, nrm, ost, bw, rlow, dk1, dv1, send, recv):
    D = BLOCK
    L = X * BLOCK
    W3 = 3 * L
    R = D // Z
    me = lax.axis_index("seq")
    hd = lax.axis_index("head")
    z = me // X
    x = me % X
    scale = 1.0 / math.sqrt(D)

    def xdev(d):
        return (z * X + (x + d) % X, hd)

    def zdev(d):
        return (((z + d + Z) % Z) * X + x, hd)

    def put(src, dst, phase, dev):
        c = pltpu.make_async_remote_copy(
            src_ref=src, dst_ref=dst, send_sem=send.at[phase], recv_sem=recv.at[phase],
            device_id=dev, device_id_type=MESH)
        c.start()

    def got(ref, phase):
        pltpu.make_async_copy(ref, ref, recv.at[phase]).wait()

    def sent(ref, phase):
        pltpu.make_async_copy(ref, ref, send.at[phase]).wait()

    barrier = pltpu.get_barrier_semaphore()

    def greet_z(d, c):
        pl.semaphore_signal(barrier, inc=1, device_id=zdev(d), device_id_type=MESH)
        return c

    lax.fori_loop(1, Z, greet_z, 0)

    def pdev(i):
        return (z * X + (x + i // H) % X, (hd + i % H) % H)

    def greet_p(i, c):
        pl.semaphore_signal(barrier, inc=1, device_id=pdev(i), device_id_type=MESH)
        return c

    lax.fori_loop(1, X * H, greet_p, 0)
    pl.semaphore_wait(barrier, (Z - 1) + (X * H - 1))

    def exchange(src, dst, base, phase):
        for d in range(1, X):
            put(src.at[(x + d) % X], dst.at[base + x], phase, xdev(d))
        dst[base + x] = src[x]

    exchange(ld, ldb, 0, LD)
    exchange(k1, k1b, 0, K1)
    exchange(v1, v1b, 0, V1)
    exchange(k2, kall, 2 * X, K2)
    exchange(q2, qall, 0, Q2)
    exchange(go, gall, 0, GO)
    exchange(q1, q1b, 0, Q1)

    rows = lax.broadcasted_iota(jnp.int32, (D, D), 0)
    cols = lax.broadcasted_iota(jnp.int32, (D, D), 1)
    eye = rows == cols

    def to_row(col):
        return jnp.sum(jnp.where(eye, col, 0.0), axis=0, keepdims=True)

    def to_col(row):
        return jnp.sum(jnp.where(eye, row, 0.0), axis=1, keepdims=True)

    got(ldb.at[pl.ds(0, X - 1)], LD)
    offset = jnp.zeros((1, 1), F32)
    for b in range(X):
        row = ldb[b]
        col = jnp.sum(jnp.where(cols <= rows, row, 0.0), axis=1, keepdims=True) + offset
        gcol[b] = col
        grow[b] = to_row(col)
        offset = offset + jnp.sum(row, axis=1, keepdims=True)
    g_end = offset
    arow[...] = jnp.broadcast_to(jnp.exp(g_end), (1, D))

    got(k1b.at[pl.ds(0, X - 1)], K1)
    got(v1b.at[pl.ds(0, X - 1)], V1)

    def add_state(b, s):
        vd = v1b[b].astype(F32) * jnp.exp(g_end - gcol[b])
        return s + dot_r(k1b[b], vd, TN)

    state = lax.fori_loop(0, X, add_state, jnp.zeros((D, D), F32))
    sst[...] = state.reshape(Z, R, D)

    def scan_send(src, dst, phase):
        def one(d, c):
            to = (z + d) % Z
            put(src.at[to], dst.at[z], phase, zdev(d))
            return c
        lax.fori_loop(1, Z, one, 0)
        dst[z] = src[z]

    scan_send(sst, sbuf, SC1)

    def decay_send(d, c):
        put(arow, abuf.at[z], DEC, zdev(d))
        return c

    lax.fori_loop(1, Z, decay_send, 0)
    abuf[z] = arow[...]

    own_k = kall.at[pl.ds(2 * X, X)]
    own_q = qall.at[pl.ds(0, X)]
    own_g = gall.at[pl.ds(0, X)]
    got(kall.at[pl.ds(0, X - 1)], K2)
    put(own_k, kall.at[pl.ds(X, X)], KA, zdev(1))
    put(own_k, kall.at[pl.ds(0, X)], KB, zdev(2))
    got(qall.at[pl.ds(0, X - 1)], Q2)
    got(gall.at[pl.ds(0, X - 1)], GO)
    put(own_q, qall.at[pl.ds(X, X)], QA, zdev(-1))
    put(own_g, gall.at[pl.ds(X, X)], GA, zdev(-1))
    put(own_q, qall.at[pl.ds(2 * X, X)], QB, zdev(-2))
    put(own_g, gall.at[pl.ds(2 * X, X)], GB, zdev(-2))

    got(q1b.at[pl.ds(0, X - 1)], Q1)
    g_row = jnp.concatenate([grow[b] for b in range(X)], axis=1)
    u_pos = lax.broadcasted_iota(jnp.int32, (D, L), 1)
    t_off = lax.broadcasted_iota(jnp.int32, (D, L), 0)
    k1all = k1b[...].reshape(L, D)
    v1all = v1b[...].reshape(L, D)

    def inner(b, c):
        low = u_pos <= t_off + b * D
        gap = gcol[b] - g_row
        w = jnp.where(low, jnp.exp(jnp.where(low, gap, 0.0)), 0.0)
        wts[b] = w
        a = dot(q1b[b], k1all, NT) * w
        aw[b] = a
        raw[b] = dot_l(a, v1all, NN)
        return c

    lax.fori_loop(0, X, inner, 0)

    def scan_local(backward, pieces, results):
        m = jnp.zeros((R, D), F32)
        for i in range(Z):
            at = Z - 1 - i if backward else i
            results[at] = m
            m = abuf[at] * m + pieces[at]

    got(sbuf.at[pl.ds(0, Z - 1)], SC1)
    got(abuf.at[pl.ds(0, Z - 1)], DEC)
    scan_local(False, sbuf, mst)
    scan_send(mst, mbuf, SC2)

    def doc_row(first):
        parts = []
        for j in range(3 * X):
            at = first + j
            inside = (at >= 0) & (at < Z * X)
            value = docs[jnp.clip(at, 0, Z * X - 1)]
            parts.append(jnp.full((1, D), jnp.where(inside, value, -1), jnp.int32))
        return jnp.concatenate(parts, axis=1)

    wide = lax.broadcasted_iota(jnp.int32, (D, W3), 1)
    tall = lax.broadcasted_iota(jnp.int32, (D, W3), 0)
    key_docs = doc_row((z - 2) * X)
    query_docs = doc_row(z * X)

    got(kall.at[pl.ds(X, X)], KA)
    got(kall.at[pl.ds(0, X)], KB)

    def probs(b, c):
        s = dot(qall[b], kall[...].reshape(W3, D), NT) * scale
        ok = (key_docs == docs[z * X + b]) & (wide <= tall + (2 * L + b * D))
        s = jnp.where(ok, s, FLOOR)
        peak = jnp.max(s, axis=1, keepdims=True)
        mass = jnp.sum(jnp.where(ok, jnp.exp(s - peak), 0.0), axis=1, keepdims=True)
        lse = peak + jnp.log(mass)
        pf[b] = jnp.where(ok, jnp.exp(s - lse), 0.0)
        lser[b] = to_row(lse)
        return c

    lax.fori_loop(0, X, probs, 0)
    put(lser, lsall.at[pl.ds(X, X)], LA, zdev(-1))
    put(lser, lsall.at[pl.ds(2 * X, X)], LB, zdev(-2))
    lsall[pl.ds(0, X)] = lser[...]

    got(qall.at[pl.ds(X, X)], QA)
    got(qall.at[pl.ds(2 * X, X)], QB)
    got(gall.at[pl.ds(X, X)], GA)
    got(gall.at[pl.ds(2 * X, X)], GB)
    got(lsall.at[pl.ds(X, X)], LA)
    got(lsall.at[pl.ds(2 * X, X)], LB)
    lse_row = jnp.concatenate([lsall[j] for j in range(3 * X)], axis=1)

    def probs_t(b, c):
        s = dot(kall[2 * X + b], qall[...].reshape(W3, D), NT) * scale
        ok = (query_docs == docs[z * X + b]) & (wide >= tall + b * D)
        p = jnp.where(ok, jnp.exp(jnp.where(ok, s - lse_row, 0.0)), 0.0)
        pt[b] = p
        gv[b] = dot(p.astype(BF16), gall[...].reshape(W3, D), NN)
        return c

    lax.fori_loop(0, X, probs_t, 0)

    got(mbuf.at[pl.ds(0, Z - 1)], SC2)
    m_state = mbuf[...].reshape(D, D)

    def outer(b, c):
        r = raw[b] + jnp.exp(gcol[b]) * dot_r(q1b[b], m_state, NN)
        raw[b] = r
        pls[b] = to_row(jnp.sum(r * r, axis=1, keepdims=True))
        pls[X + b] = to_row(jnp.sum(r * gv[b], axis=1, keepdims=True))
        return c

    lax.fori_loop(0, X, outer, 0)

    def plane_send(i, c):
        put(pls, plb.at[i], PLN, pdev(i))
        return c

    lax.fori_loop(1, X * H, plane_send, 0)
    plb[0] = pls[...]
    got(plb.at[pl.ds(1, X * H - 1)], PLN)
    sums = jnp.sum(plb[...], axis=0)
    inv_row = 1.0 / jnp.sqrt(sums[:X] / width_all + NORM_EPSILON)
    coef_row = inv_row * inv_row * inv_row * sums[X:] / width_all
    nrm[pl.ds(0, X)] = inv_row
    nrm[pl.ds(X, X)] = coef_row

    def finish(b, d_state):
        inv = to_col(nrm[b])
        coef = to_col(nrm[X + b])
        r = raw[b]
        vall[2 * X + b] = (r * inv).astype(BF16)
        g = inv * gv[b] - r * coef
        rr[b] = g
        return d_state + dot_r(q1b[b], g * jnp.exp(gcol[b]), TN)

    d_state = lax.fori_loop(0, X, finish, jnp.zeros((D, D), F32))
    sst2[...] = d_state.reshape(Z, R, D)
    scan_send(sst2, sbuf2, SC3)
    own_v = vall.at[pl.ds(2 * X, X)]
    put(own_v, vall.at[pl.ds(X, X)], VA, zdev(1))
    put(own_v, vall.at[pl.ds(0, X)], VB, zdev(2))

    def give_back(n, out, phase):
        for d in range(1, X):
            put(ost.at[n, (x + d) % X], out.at[x], phase, xdev(d))
        out[x] = ost[n, x]

    m_low = m_state.astype(BF16)

    def inner_q(b, c):
        g = rr[b].astype(BF16)
        back = (dot(g, v1all, NT) * wts[b]).astype(BF16)
        bw[b] = back
        rlow[b] = g
        part = dot(back, k1all, NN) + jnp.exp(gcol[b]) * dot(g, m_low, NT)
        ost[0, b] = part.astype(BF16)
        return c

    lax.fori_loop(0, X, inner_q, 0)
    give_back(0, o_q1, O0)
    q1all = q1b[...].reshape(L, D)
    rall = rlow[...].reshape(L, D)
    for b in range(X):
        own = pl.ds(b * D, D)
        dk1[b] = dot(bw[:, :, own].reshape(L, D), q1all, TN)
        dv1[b] = dot(aw[:, :, own].reshape(L, D).astype(BF16), rall, TN)

    got(sbuf2.at[pl.ds(0, Z - 1)], SC3)
    scan_local(True, sbuf2, mst2)
    scan_send(mst2, mbuf2, SC4)

    got(vall.at[pl.ds(X, X)], VA)
    got(vall.at[pl.ds(0, X)], VB)

    def query_grads(b, c):
        p = pf[b]
        gp = dot(gall[b], vall[...].reshape(W3, D), NT)
        delta = jnp.sum(p.astype(BF16).astype(F32) * gp, axis=1, keepdims=True)
        delr[b] = to_row(delta)
        ds = (p * (gp - delta) * scale).astype(BF16)
        ost[3, b] = dot(ds, kall[...].reshape(W3, D), NN).astype(BF16)
        return c

    lax.fori_loop(0, X, query_grads, 0)
    put(delr, dlall.at[pl.ds(X, X)], DA, zdev(-1))
    put(delr, dlall.at[pl.ds(2 * X, X)], DB, zdev(-2))
    dlall[pl.ds(0, X)] = delr[...]
    give_back(3, o_q2, O3)

    got(dlall.at[pl.ds(X, X)], DA)
    got(dlall.at[pl.ds(2 * X, X)], DB)
    delta_row = jnp.concatenate([dlall[j] for j in range(3 * X)], axis=1)

    def key_grads(b, c):
        gp = dot(vall[2 * X + b], gall[...].reshape(W3, D), NT)
        ds = (pt[b] * (gp - delta_row) * scale).astype(BF16)
        ost[4, b] = dot(ds, qall[...].reshape(W3, D), NN).astype(BF16)
        return c

    lax.fori_loop(0, X, key_grads, 0)
    give_back(4, o_k2, O4)

    got(mbuf2.at[pl.ds(0, Z - 1)], SC4)
    later = mbuf2[...].reshape(D, D).astype(BF16)

    def state_grads(b, c):
        tail = jnp.exp(g_end - gcol[b])
        ost[1, b] = (dk1[b] + tail * dot(v1b[b], later, NT)).astype(BF16)
        ost[2, b] = (dv1[b] + tail * dot(k1b[b], later, NN)).astype(BF16)
        return c

    lax.fori_loop(0, X, state_grads, 0)
    give_back(1, o_k1, O1)
    give_back(2, o_v1, O2)

    for out, phase in ((o_q1, O0), (o_k1, O1), (o_v1, O2), (o_q2, O3), (o_k2, O4)):
        got(out.at[pl.ds(0, X - 1)], phase)
        sent(out.at[pl.ds(0, X - 1)], phase)
    for ref, phase in ((ldb, LD), (k1b, K1), (v1b, V1), (kall, K2), (qall, Q2), (gall, GO), (q1b, Q1)):
        sent(ref.at[pl.ds(0, X - 1)], phase)
    for ref, phase in ((sbuf, SC1), (abuf, DEC), (mbuf, SC2), (sbuf2, SC3), (mbuf2, SC4)):
        sent(ref.at[pl.ds(0, Z - 1)], phase)
    for ref, phase in ((kall, KA), (kall, KB), (qall, QA), (qall, QB), (gall, GA), (gall, GB),
                       (lser, LA), (lser, LB), (vall, VA), (vall, VB), (delr, DA), (delr, DB)):
        sent(ref.at[pl.ds(0, X)], phase)
    sent(plb.at[pl.ds(1, X * H - 1)], PLN)


def make_body(Z, X, H):
    D = BLOCK

    def vm(*shape, dtype=F32):
        return pltpu.VMEM(shape, dtype)

    def body(q1, k1, v1, ld, q2, k2, go, docs):
        heads_first = [jnp.transpose(a, (1, 0, 2)) for a in (q1, k1, v1, q2, k2, go)]
        L = X * D
        blocks = jax.ShapeDtypeStruct((X, D, D), BF16)
        low = functools.partial(vm, dtype=BF16)
        scratch = [
            low(X, D, D), low(X, D, D), low(X, D, D),
            low(3 * X, D, D), low(3 * X, D, D), low(3 * X, D, D), low(3 * X, D, D),
            vm(X, 1, D), vm(X, D, 1), vm(X, 1, D),
            vm(X, D, L), vm(X, D, L), vm(X, D, 3 * L), vm(X, D, 3 * L),
            vm(X, 1, D), vm(X, 1, D), vm(3 * X, 1, D), vm(3 * X, 1, D),
            vm(Z, D // Z, D), vm(Z, D // Z, D), vm(Z, D // Z, D), vm(Z, D // Z, D),
            vm(Z, D // Z, D), vm(Z, D // Z, D), vm(Z, D // Z, D), vm(Z, D // Z, D),
            vm(Z, 1, D), vm(1, D),
            vm(X, D, D), vm(X, D, D), vm(X, D, D),
            vm(2 * X, 1, D), vm(X * H, 2 * X, 1, D), vm(2 * X, 1, D),
            low(5, X, D, D), low(X, D, L), low(X, D, D), vm(X, D, D), vm(X, D, D),
            pltpu.SemaphoreType.DMA((NSEM,)), pltpu.SemaphoreType.DMA((NSEM,)),
        ]
        vmem = pl.BlockSpec(memory_space=pltpu.VMEM)
        outs = pl.pallas_call(
            functools.partial(kernel, Z, X, H, float(X * H * D)),
            out_shape=[blocks] * 5,
            in_specs=[vmem] * 7 + [pl.BlockSpec(memory_space=pltpu.SMEM)],
            out_specs=[vmem] * 5,
            scratch_shapes=scratch,
            compiler_params=pltpu.CompilerParams(
                collective_id=0, has_side_effects=True, vmem_limit_bytes=60 * 1024 * 1024),
        )(*heads_first, ld.reshape(X, 1, D), docs)
        return tuple(jnp.transpose(o, (1, 0, 2)).astype(F32) for o in outs)

    return body


def solution(mesh):
    split_both = P("seq", "head", None)
    placed = (split_both,) * 3 + (P("head", "seq"),) + (split_both,) * 3 + (P(),)
    return jax.shard_map(
        make_body(mesh.shape["seq"] // ROW, ROW, mesh.shape["head"]),
        mesh=mesh,
        in_specs=placed,
        out_specs=(split_both,) * 5,
        check_vma=False,
    )
```

```python
import functools
import math

import jax
import jax.numpy as jnp
from jax import lax
from jax.experimental import pallas as pl
from jax.experimental.pallas import tpu as pltpu
from jax.sharding import PartitionSpec as P

BLOCK = 128
ROW = 4
NORM_EPSILON = 1e-05
FLOOR = -1e30
MESH = pl.DeviceIdType.MESH
F32 = jnp.float32
BF16 = jnp.bfloat16

(LD, K1, V1, K2, Q2, GO, Q1, TL, SC1, DEC, SC2, KA, KB, QA, QB, GA, GB, LA, LB, PLN,
 SC3, SC4, VA, VB, VC, VD, DA, DB, O0, O1, O2, O3, O4, LG) = range(34)
NSEM = 34

NN = (((1,), (0,)), ((), ()))
NT = (((1,), (1,)), ((), ()))
TN = (((0,), (0,)), ((), ()))


def dot(a, b, dims):
    return lax.dot_general(a, b, dims, preferred_element_type=F32)


def split(a):
    high = a.astype(BF16)
    return high, (a - high.astype(F32)).astype(BF16)


def dot_l(a, b, dims):
    high, low = split(a)
    return dot(high, b, dims) + dot(low, b, dims)


def dot_r(a, b, dims):
    high, low = split(b)
    return dot(a, high, dims) + dot(a, low, dims)


def kernel(Z, X, H, width_all, q1_in, k1_in, v1_in, q2_in, k2_in, go_in, ld, docs,
           o_q1, o_k1, o_v1, o_q2, o_k2,
           raw_in, wide_in, hm, q1b, k1b, v1b, kall, qall, gall, vall, ldb, gcol, grow,
           wts, aw, pf, pt, lser, delr, lsall, dlall, kdoc, qdoc,
           sst, sbuf, mst, mbuf, sst2, sbuf2, mst2, mbuf2, abuf, arow,
           raw, gv, rr, pls, plb, nrm, ost, pk1, pv1, bw, rlow, dk1, dv1,
           tails, tailb, lgs, lgb, send, recv, load):
    D = BLOCK
    L = X * BLOCK
    W2 = 2 * L
    R = D // Z
    me = lax.axis_index("seq")
    hd = lax.axis_index("head")
    z = me // X
    x = me % X
    scale = 1.0 / math.sqrt(D)

    def xdev(d):
        return (z * X + (x + d) % X, hd)

    def zdev(d):
        return (((z + d + Z) % Z) * X + x, hd)

    def put(src, dst, phase, dev):
        c = pltpu.make_async_remote_copy(
            src_ref=src, dst_ref=dst, send_sem=send.at[phase], recv_sem=recv.at[phase],
            device_id=dev, device_id_type=MESH)
        c.start()

    def got(ref, phase):
        pltpu.make_async_copy(ref, ref, recv.at[phase]).wait()

    def sent(ref, phase):
        pltpu.make_async_copy(ref, ref, send.at[phase]).wait()

    barrier = pltpu.get_barrier_semaphore()

    def greet_z(d, c):
        pl.semaphore_signal(barrier, inc=1, device_id=zdev(d), device_id_type=MESH)
        return c

    lax.fori_loop(1, Z, greet_z, 0)

    def pdev(i):
        return (z * X + (x + i // H) % X, (hd + i % H) % H)

    def greet_p(i, c):
        pl.semaphore_signal(barrier, inc=1, device_id=pdev(i), device_id_type=MESH)
        return c

    lax.fori_loop(1, X * H, greet_p, 0)

    sources = (k1_in, v1_in, k2_in, q2_in, go_in, q1_in)
    for n, src in enumerate(sources):
        pltpu.make_async_copy(src, raw_in.at[n], load.at[n]).start()
    for n, src in enumerate(sources):
        pltpu.make_async_copy(src, raw_in.at[n], load.at[n]).wait()
        wide_in[...] = raw_in[n].astype(F32)
        for h in range(X):
            hm[n, h] = wide_in[:, h, :].astype(BF16)
    pl.semaphore_wait(barrier, (Z - 1) + (X * H - 1))

    def exchange(src, dst, base, phase):
        for d in range(1, X):
            put(src.at[(x + d) % X], dst.at[base + x], phase, xdev(d))
        dst[base + x] = src[x]

    exchange(ld, ldb, 0, LD)
    exchange(hm.at[0], k1b, 0, K1)
    exchange(hm.at[1], v1b, 0, V1)
    exchange(hm.at[2], kall, 2 * X, K2)
    exchange(hm.at[3], qall, 0, Q2)
    exchange(hm.at[4], gall, 0, GO)
    exchange(hm.at[5], q1b, 0, Q1)

    rows = lax.broadcasted_iota(jnp.int32, (D, D), 0)
    cols = lax.broadcasted_iota(jnp.int32, (D, D), 1)
    eye = rows == cols

    def to_row(col):
        return jnp.sum(jnp.where(eye, col, 0.0), axis=0, keepdims=True)

    def to_col(row):
        return jnp.sum(jnp.where(eye, row, 0.0), axis=1, keepdims=True)

    got(ldb.at[pl.ds(0, X - 1)], LD)
    offset = jnp.zeros((1, 1), F32)
    for b in range(X):
        row = ldb[b]
        col = jnp.sum(jnp.where(cols <= rows, row, 0.0), axis=1, keepdims=True) + offset
        gcol[b] = col
        grow[b] = to_row(col)
        offset = offset + jnp.sum(row, axis=1, keepdims=True)
    g_end = offset
    arow[...] = jnp.broadcast_to(jnp.exp(g_end), (1, D))
    for b in range(X):
        tails[b] = jnp.exp(g_end - grow[b])

    got(k1b.at[pl.ds(0, X - 1)], K1)
    got(v1b.at[pl.ds(0, X - 1)], V1)

    def add_state(b, s):
        vd = v1b[b].astype(F32) * jnp.exp(g_end - gcol[b])
        return s + dot_r(k1b[b], vd, TN)

    state = lax.fori_loop(0, X, add_state, jnp.zeros((D, D), F32))
    sst[...] = state.reshape(Z, R, D)

    def scan_send(src, dst, phase):
        def one(d, c):
            to = (z + d) % Z
            put(src.at[to], dst.at[z], phase, zdev(d))
            return c
        lax.fori_loop(1, Z, one, 0)
        dst[z] = src[z]

    scan_send(sst, sbuf, SC1)

    def decay_send(d, c):
        put(arow, abuf.at[z], DEC, zdev(d))
        return c

    lax.fori_loop(1, Z, decay_send, 0)
    abuf[z] = arow[...]

    got(kall.at[pl.ds(0, X - 1)], K2)
    put(kall.at[pl.ds(2 * X, X)], kall.at[pl.ds(X, X)], KA, zdev(1))
    got(qall.at[pl.ds(0, X - 1)], Q2)
    put(qall.at[pl.ds(0, X)], qall.at[pl.ds(X, X)], QA, zdev(-1))
    got(gall.at[pl.ds(0, X - 1)], GO)
    put(gall.at[pl.ds(0, X)], gall.at[pl.ds(X, X)], GA, zdev(-1))
    exchange(tails, tailb, 0, TL)

    got(q1b.at[pl.ds(0, X - 1)], Q1)
    g_row = jnp.concatenate([grow[b] for b in range(X)], axis=1)
    u_pos = lax.broadcasted_iota(jnp.int32, (D, L), 1)
    t_off = lax.broadcasted_iota(jnp.int32, (D, L), 0)
    k1all = k1b[...].reshape(L, D)
    v1all = v1b[...].reshape(L, D)

    def inner(b, c):
        low = u_pos <= t_off + b * D
        gap = gcol[b] - g_row
        w = jnp.where(low, jnp.exp(jnp.where(low, gap, 0.0)), 0.0)
        wts[b] = w
        a = dot(q1b[b], k1all, NT) * w
        aw[b] = a
        raw[b] = dot_l(a, v1all, NN)
        return c

    lax.fori_loop(0, X, inner, 0)

    for j in range(3 * X):
        for ref, first in ((kdoc, (z - 2) * X), (qdoc, z * X)):
            at = first + j
            inside = (at >= 0) & (at < Z * X)
            value = docs[jnp.clip(at, 0, Z * X - 1)]
            ref[j] = jnp.full((1, D), jnp.where(inside, value, -1), jnp.int32)

    got(kall.at[pl.ds(X, X)], KA)
    put(kall.at[pl.ds(X + 1, X - 1)], kall.at[pl.ds(1, X - 1)], KB, zdev(1))
    got(qall.at[pl.ds(X, X)], QA)
    put(qall.at[pl.ds(X, X - 1)], qall.at[pl.ds(2 * X, X - 1)], QB, zdev(-1))

    def scan_local(backward, pieces, results):
        m = jnp.zeros((R, D), F32)
        for i in range(Z):
            at = Z - 1 - i if backward else i
            results[at] = m
            m = abuf[at] * m + pieces[at]

    got(sbuf.at[pl.ds(0, Z - 1)], SC1)
    got(abuf.at[pl.ds(0, Z - 1)], DEC)
    scan_local(False, sbuf, mst)
    scan_send(mst, mbuf, SC2)
    got(gall.at[pl.ds(X, X)], GA)
    put(gall.at[pl.ds(X, X - 1)], gall.at[pl.ds(2 * X, X - 1)], GB, zdev(-1))

    wide = lax.broadcasted_iota(jnp.int32, (D, W2), 1)
    tall = lax.broadcasted_iota(jnp.int32, (D, W2), 0)

    def window(ref, first):
        return ref[pl.ds(first, 2 * X)].reshape(W2, D)

    def window_row(ref, first):
        return jnp.concatenate([ref[first + i] for i in range(2 * X)], axis=1)

    got(kall.at[pl.ds(1, X - 1)], KB)

    def probs(b, c):
        s = dot(qall[b], window(kall, b + 1), NT) * scale
        ok = (window_row(kdoc, b + 1) == docs[z * X + b]) & (wide <= tall + (W2 - D))
        s = jnp.where(ok, s, FLOOR)
        peak = jnp.max(s, axis=1, keepdims=True)
        mass = jnp.sum(jnp.where(ok, jnp.exp(s - peak), 0.0), axis=1, keepdims=True)
        lse = peak + jnp.log(mass)
        pf[b] = jnp.where(ok, jnp.exp(s - lse), 0.0)
        lser[b] = to_row(lse)
        return c

    lax.fori_loop(0, X, probs, 0)
    put(lser, lsall.at[pl.ds(X, X)], LA, zdev(-1))
    put(lser, lsall.at[pl.ds(2 * X, X)], LB, zdev(-2))
    lsall[pl.ds(0, X)] = lser[...]

    got(qall.at[pl.ds(2 * X, X - 1)], QB)
    got(gall.at[pl.ds(2 * X, X - 1)], GB)
    got(lsall.at[pl.ds(X, X)], LA)
    got(lsall.at[pl.ds(2 * X, X)], LB)

    def probs_t(b, c):
        s = dot(kall[2 * X + b], window(qall, b), NT) * scale
        ok = (window_row(qdoc, b) == docs[z * X + b]) & (wide >= tall)
        p = jnp.where(ok, jnp.exp(jnp.where(ok, s - window_row(lsall, b), 0.0)), 0.0)
        pt[b] = p
        gv[b] = dot(p.astype(BF16), window(gall, b), NN)
        return c

    lax.fori_loop(0, X, probs_t, 0)

    got(mbuf.at[pl.ds(0, Z - 1)], SC2)
    m_state = mbuf[...].reshape(D, D)

    def outer(b, c):
        r = raw[b] + jnp.exp(gcol[b]) * dot_r(q1b[b], m_state, NN)
        raw[b] = r
        pls[b] = to_row(jnp.sum(r * r, axis=1, keepdims=True))
        pls[X + b] = to_row(jnp.sum(r * gv[b], axis=1, keepdims=True))
        return c

    lax.fori_loop(0, X, outer, 0)

    def plane_send(i, c):
        put(pls, plb.at[i], PLN, pdev(i))
        return c

    lax.fori_loop(1, X * H, plane_send, 0)
    plb[0] = pls[...]
    got(plb.at[pl.ds(1, X * H - 1)], PLN)
    sums = jnp.sum(plb[...], axis=0)
    inv_row = 1.0 / jnp.sqrt(sums[:X] / width_all + NORM_EPSILON)
    coef_row = inv_row * inv_row * inv_row * sums[X:] / width_all
    nrm[pl.ds(0, X)] = inv_row
    nrm[pl.ds(X, X)] = coef_row

    def finish(b, d_state):
        inv = to_col(nrm[b])
        coef = to_col(nrm[X + b])
        r = raw[b]
        vall[2 * X + b] = (r * inv).astype(BF16)
        g = inv * gv[b] - r * coef
        rr[b] = g
        return d_state + dot_r(q1b[b], g * jnp.exp(gcol[b]), TN)

    d_state = lax.fori_loop(0, X, finish, jnp.zeros((D, D), F32))
    sst2[...] = d_state.reshape(Z, R, D)
    scan_send(sst2, sbuf2, SC3)
    half = X // 2
    put(vall.at[pl.ds(2 * X + half, half)], vall.at[pl.ds(X + half, half)], VA, zdev(1))
    put(vall.at[pl.ds(2 * X, half)], vall.at[pl.ds(X, half)], VB, zdev(1))

    def give_back(n, out, phase):
        for d in range(1, X):
            put(ost.at[n, (x + d) % X], out.at[x], phase, xdev(d))
        out[x] = ost[n, x]

    m_low = m_state.astype(BF16)

    def inner_q(b, c):
        g = rr[b].astype(BF16)
        back = (dot(g, v1all, NT) * wts[b]).astype(BF16)
        bw[b] = back
        rlow[b] = g
        part = dot(back, k1all, NN) + jnp.exp(gcol[b]) * dot(g, m_low, NT)
        ost[0, b] = part.astype(BF16)
        return c

    lax.fori_loop(0, X, inner_q, 0)
    got(vall.at[pl.ds(X + half, half)], VA)
    put(vall.at[pl.ds(X + half, half)], vall.at[pl.ds(half, half)], VC, zdev(1))
    give_back(0, o_q1, O0)
    q1all = q1b[...].reshape(L, D)
    rall = rlow[...].reshape(L, D)
    for b in range(X):
        own = pl.ds(b * D, D)
        ost[1, b] = dot(bw[:, :, own].reshape(L, D), q1all, TN).astype(BF16)
        ost[2, b] = dot(aw[:, :, own].reshape(L, D).astype(BF16), rall, TN).astype(BF16)
    got(vall.at[pl.ds(X, half)], VB)
    if half > 1:
        put(vall.at[pl.ds(X + 1, half - 1)], vall.at[pl.ds(1, half - 1)], VD, zdev(1))
    give_back(1, pk1, O1)
    give_back(2, pv1, O2)

    got(sbuf2.at[pl.ds(0, Z - 1)], SC3)
    scan_local(True, sbuf2, mst2)
    scan_send(mst2, mbuf2, SC4)

    got(vall.at[pl.ds(half, half)], VC)
    if half > 1:
        got(vall.at[pl.ds(1, half - 1)], VD)

    def query_grads(b, c):
        p = pf[b]
        gp = dot(gall[b], window(vall, b + 1), NT)
        delta = jnp.sum(p.astype(BF16).astype(F32) * gp, axis=1, keepdims=True)
        delr[b] = to_row(delta)
        ds = (p * (gp - delta) * scale).astype(BF16)
        ost[3, b] = dot(ds, window(kall, b + 1), NN).astype(BF16)
        return c

    lax.fori_loop(0, X, query_grads, 0)
    put(delr, dlall.at[pl.ds(X, X)], DA, zdev(-1))
    put(delr, dlall.at[pl.ds(2 * X, X)], DB, zdev(-2))
    dlall[pl.ds(0, X)] = delr[...]
    give_back(3, o_q2, O3)

    got(dlall.at[pl.ds(X, X)], DA)
    got(dlall.at[pl.ds(2 * X, X)], DB)

    def key_grads(b, c):
        gp = dot(vall[2 * X + b], window(gall, b), NT)
        ds = (pt[b] * (gp - window_row(dlall, b)) * scale).astype(BF16)
        ost[4, b] = dot(ds, window(qall, b), NN).astype(BF16)
        return c

    lax.fori_loop(0, X, key_grads, 0)
    give_back(4, o_k2, O4)

    got(pk1.at[pl.ds(0, X - 1)], O1)
    got(pv1.at[pl.ds(0, X - 1)], O2)
    got(tailb.at[pl.ds(0, X - 1)], TL)
    got(mbuf2.at[pl.ds(0, Z - 1)], SC4)
    lgs[...] = mbuf2[...].reshape(D, D).astype(BF16)
    for d in range(1, X):
        put(lgs, lgb.at[x], LG, xdev(d))
    lgb[x] = lgs[...]
    got(lgb.at[pl.ds(0, X - 1)], LG)

    def state_grads(h, c):
        tail = to_col(tailb[h])
        later = lgb[h]
        o_k1[h] = pk1[h].astype(F32) + tail * dot(hm[1, h], later, NT)
        o_v1[h] = pv1[h].astype(F32) + tail * dot(hm[0, h], later, NN)
        return c

    lax.fori_loop(0, X, state_grads, 0)

    for out, phase in ((o_q1, O0), (o_q2, O3), (o_k2, O4)):
        got(out.at[pl.ds(0, X - 1)], phase)
    for ref, phase in ((ldb, LD), (k1b, K1), (v1b, V1), (kall, K2), (qall, Q2), (gall, GO), (q1b, Q1),
                       (tailb, TL), (o_q1, O0), (pk1, O1), (pv1, O2), (o_q2, O3), (o_k2, O4), (lgb, LG)):
        sent(ref.at[pl.ds(0, X - 1)], phase)
    for ref, phase in ((sbuf, SC1), (abuf, DEC), (mbuf, SC2), (sbuf2, SC3), (mbuf2, SC4)):
        sent(ref.at[pl.ds(0, Z - 1)], phase)
    for ref, phase in ((kall, KA), (qall, QA), (gall, GA), (lser, LA), (lser, LB), (delr, DA), (delr, DB)):
        sent(ref.at[pl.ds(0, X)], phase)
    for ref, phase in ((kall, KB), (qall, QB), (gall, GB)):
        sent(ref.at[pl.ds(0, X - 1)], phase)
    for phase in (VA, VB, VC):
        sent(vall.at[pl.ds(0, half)], phase)
    if half > 1:
        sent(vall.at[pl.ds(0, half - 1)], VD)
    sent(plb.at[pl.ds(1, X * H - 1)], PLN)


def place(X, a, b, c, d, e, oa, ob, oc, od, oe):
    for src, dst in ((a, oa), (b, ob), (c, oc), (d, od), (e, oe)):
        for h in range(X):
            dst[:, h, :] = src[h].astype(F32)


def make_body(Z, X, H):
    D = BLOCK

    def vm(*shape, dtype=F32):
        return pltpu.VMEM(shape, dtype)

    def body(q1, k1, v1, ld, q2, k2, go, docs):
        L = X * D
        low_blocks = jax.ShapeDtypeStruct((X, D, D), BF16)
        blocks = jax.ShapeDtypeStruct((X, D, D), F32)
        low = functools.partial(vm, dtype=BF16)
        scratch = [
            low(6, D, X, D), vm(D, X, D), low(6, X, D, D),
            low(X, D, D), low(X, D, D), low(X, D, D),
            low(3 * X, D, D), low(3 * X, D, D), low(3 * X, D, D), low(3 * X, D, D),
            vm(X, 1, D), vm(X, D, 1), vm(X, 1, D),
            vm(X, D, L), vm(X, D, L), vm(X, D, 2 * L), vm(X, D, 2 * L),
            vm(X, 1, D), vm(X, 1, D), vm(3 * X, 1, D), vm(3 * X, 1, D),
            vm(3 * X, 1, D, dtype=jnp.int32), vm(3 * X, 1, D, dtype=jnp.int32),
            vm(Z, D // Z, D), vm(Z, D // Z, D), vm(Z, D // Z, D), vm(Z, D // Z, D),
            vm(Z, D // Z, D), vm(Z, D // Z, D), vm(Z, D // Z, D), vm(Z, D // Z, D),
            vm(Z, 1, D), vm(1, D),
            vm(X, D, D), vm(X, D, D), vm(X, D, D),
            vm(2 * X, 1, D), vm(X * H, 2 * X, 1, D), vm(2 * X, 1, D),
            low(5, X, D, D), low(X, D, D), low(X, D, D),
            low(X, D, L), low(X, D, D), vm(X, D, D), vm(X, D, D),
            vm(X, 1, D), vm(X, 1, D), low(D, D), low(X, D, D),
            pltpu.SemaphoreType.DMA((NSEM,)), pltpu.SemaphoreType.DMA((NSEM,)),
            pltpu.SemaphoreType.DMA((6,)),
        ]
        vmem = pl.BlockSpec(memory_space=pltpu.VMEM)
        anywhere = pl.BlockSpec(memory_space=pl.ANY)
        outs = pl.pallas_call(
            functools.partial(kernel, Z, X, H, float(X * H * D)),
            out_shape=[low_blocks, blocks, blocks, low_blocks, low_blocks],
            in_specs=[anywhere] * 6 + [vmem, pl.BlockSpec(memory_space=pltpu.SMEM)],
            out_specs=[vmem] * 5,
            scratch_shapes=scratch,
            compiler_params=pltpu.CompilerParams(
                collective_id=0, has_side_effects=True, vmem_limit_bytes=60 * 1024 * 1024),
        )(q1, k1, v1, q2, k2, go, ld.reshape(X, 1, D), docs)
        return tuple(pl.pallas_call(
            functools.partial(place, X),
            out_shape=[jax.ShapeDtypeStruct((D, X, D), F32)] * 5,
            in_specs=[vmem] * 5,
            out_specs=[vmem] * 5,
        )(*outs))

    return body


def solution(mesh):
    split_both = P("seq", "head", None)
    placed = (split_both,) * 3 + (P("head", "seq"),) + (split_both,) * 3 + (P(),)
    return jax.shard_map(
        make_body(mesh.shape["seq"] // ROW, ROW, mesh.shape["head"]),
        mesh=mesh,
        in_specs=placed,
        out_specs=(split_both,) * 5,
        check_vma=False,
    )
```

```python
import functools
import math

import jax
import jax.numpy as jnp
from jax import lax
from jax.experimental import pallas as pl
from jax.experimental.pallas import tpu as pltpu
from jax.sharding import PartitionSpec as P

BLOCK = 128
ROW = 4
NORM_EPSILON = 1e-05
FLOOR = -1e30
MESH = pl.DeviceIdType.MESH
F32 = jnp.float32
BF16 = jnp.bfloat16

(LD, K1, V1, K2, Q2, GO, Q1, TL, SC1, DEC, SC2, KA, KB, QA, QB, GA, GB, LA, LB, PLN,
 SC3, SC4, VA, VB, VC, VD, DA, DB, O0, O1, O2, O3, O4, LG) = range(34)
NSEM = 34

NN = (((1,), (0,)), ((), ()))
NT = (((1,), (1,)), ((), ()))
TN = (((0,), (0,)), ((), ()))


def dot(a, b, dims):
    return lax.dot_general(a, b, dims, preferred_element_type=F32)


def split(a):
    high = a.astype(BF16)
    return high, (a - high.astype(F32)).astype(BF16)


def dot_l(a, b, dims):
    high, low = split(a)
    return dot(high, b, dims) + dot(low, b, dims)


def dot_r(a, b, dims):
    high, low = split(b)
    return dot(a, high, dims) + dot(a, low, dims)


def kernel(Z, X, H, width_all, q1_in, k1_in, v1_in, q2_in, k2_in, go_in, ld_in, docs_in,
           o_q1, o_k1, o_v1, o_q2, o_k2,
           raw_in, wide_in, hm, q1b, k1b, v1b, kall, qall, gall, vall, ldb, gcol, grow,
           wts, aw, pf, pt, lser, delr, lsall, dlall, kdoc, qdoc,
           sst, sbuf, mst, mbuf, sst2, sbuf2, mst2, mbuf2, abuf, arow,
           raw, gv, rr, pls, plb, nrm, ost, pk1, pv1, bw, rlow, dk1, dv1,
           tails, tailb, lgs, lgb, ld, docs, invc, send, recv, load):
    D = BLOCK
    L = X * BLOCK
    W2 = 2 * L
    R = D // Z
    me = lax.axis_index("seq")
    hd = lax.axis_index("head")
    z = me // X
    x = me % X
    scale = 1.0 / math.sqrt(D)

    def xdev(d):
        return (z * X + (x + d) % X, hd)

    def zdev(d):
        return (((z + d + Z) % Z) * X + x, hd)

    def put(src, dst, phase, dev):
        c = pltpu.make_async_remote_copy(
            src_ref=src, dst_ref=dst, send_sem=send.at[phase], recv_sem=recv.at[phase],
            device_id=dev, device_id_type=MESH)
        c.start()

    def got(ref, phase):
        pltpu.make_async_copy(ref, ref, recv.at[phase]).wait()

    def sent(ref, phase):
        pltpu.make_async_copy(ref, ref, send.at[phase]).wait()

    barrier = pltpu.get_barrier_semaphore()

    def greet_z(d, c):
        pl.semaphore_signal(barrier, inc=1, device_id=zdev(d), device_id_type=MESH)
        return c

    lax.fori_loop(1, Z, greet_z, 0)

    def pdev(i):
        return (z * X + (x + i // H) % X, (hd + i % H) % H)

    def greet_p(i, c):
        pl.semaphore_signal(barrier, inc=1, device_id=pdev(i), device_id_type=MESH)
        return c

    lax.fori_loop(1, X * H, greet_p, 0)

    sources = (k1_in, v1_in, k2_in, q2_in, go_in, q1_in)
    for n, src in enumerate(sources):
        pltpu.make_async_copy(src, raw_in.at[n], load.at[n]).start()
    pltpu.make_async_copy(ld_in, ld, load.at[6]).start()
    pltpu.make_async_copy(docs_in, docs, load.at[7]).start()
    for n, src in enumerate(sources):
        pltpu.make_async_copy(src, raw_in.at[n], load.at[n]).wait()
        wide_in[...] = raw_in[n].astype(F32)
        for h in range(X):
            hm[n, h] = wide_in[:, h, :].astype(BF16)
    pltpu.make_async_copy(ld_in, ld, load.at[6]).wait()
    pltpu.make_async_copy(docs_in, docs, load.at[7]).wait()
    pl.semaphore_wait(barrier, (Z - 1) + (X * H - 1))

    def exchange(src, dst, base, phase):
        for d in range(1, X):
            put(src.at[(x + d) % X], dst.at[base + x], phase, xdev(d))
        dst[base + x] = src[x]

    exchange(ld, ldb, 0, LD)
    exchange(hm.at[0], k1b, 0, K1)
    exchange(hm.at[1], v1b, 0, V1)
    put(hm.at[3, x], qall.at[X + x], QA, zdev(-1))
    put(hm.at[2, x], kall.at[X + x], KA, zdev(1))
    put(hm.at[4, x], gall.at[X + x], GA, zdev(-1))
    exchange(hm.at[3], qall, 0, Q2)
    exchange(hm.at[2], kall, 2 * X, K2)
    exchange(hm.at[4], gall, 0, GO)
    exchange(hm.at[5], q1b, 0, Q1)

    rows = lax.broadcasted_iota(jnp.int32, (D, D), 0)
    cols = lax.broadcasted_iota(jnp.int32, (D, D), 1)
    eye = rows == cols

    def to_row(col):
        return jnp.sum(jnp.where(eye, col, 0.0), axis=0, keepdims=True)

    def to_col(row):
        return jnp.sum(jnp.where(eye, row, 0.0), axis=1, keepdims=True)

    got(ldb.at[pl.ds(0, X - 1)], LD)
    offset = jnp.zeros((1, 1), F32)
    for b in range(X):
        row = ldb[b]
        col = jnp.sum(jnp.where(cols <= rows, row, 0.0), axis=1, keepdims=True) + offset
        gcol[b] = col
        grow[b] = to_row(col)
        offset = offset + jnp.sum(row, axis=1, keepdims=True)
    g_end = offset
    arow[...] = jnp.broadcast_to(jnp.exp(g_end), (1, D))
    for b in range(X):
        tails[b] = jnp.exp(g_end - grow[b])

    got(k1b.at[pl.ds(0, X - 1)], K1)
    got(v1b.at[pl.ds(0, X - 1)], V1)

    def add_state(b, s):
        vd = v1b[b].astype(F32) * jnp.exp(g_end - gcol[b])
        return s + dot_r(k1b[b], vd, TN)

    state = lax.fori_loop(0, X, add_state, jnp.zeros((D, D), F32))
    sst[...] = state.reshape(Z, R, D).astype(BF16)

    def far_first(i):
        return Z // 2 + ((i + 1) // 2) * (2 * (i % 2) - 1)

    def scan_send(src, dst, phase):
        def one(i, c):
            d = far_first(i)
            to = (z + d) % Z
            put(src.at[to], dst.at[z], phase, zdev(d))
            return c
        lax.fori_loop(0, Z - 1, one, 0)
        dst[z] = src[z]

    scan_send(sst, sbuf, SC1)

    def decay_send(i, c):
        put(arow, abuf.at[z], DEC, zdev(far_first(i)))
        return c

    lax.fori_loop(0, Z - 1, decay_send, 0)
    abuf[z] = arow[...]

    def pass_on(ref, base, phase, dev):
        for d in range(1, X):
            at = (x + d) % X
            put(ref.at[base + at], ref.at[X + at], phase, dev)

    got(qall.at[pl.ds(0, X - 1)], Q2)
    pass_on(qall, 0, QA, zdev(-1))
    got(kall.at[pl.ds(0, X - 1)], K2)
    pass_on(kall, 2 * X, KA, zdev(1))
    got(gall.at[pl.ds(0, X - 1)], GO)
    pass_on(gall, 0, GA, zdev(-1))
    exchange(tails, tailb, 0, TL)

    got(q1b.at[pl.ds(0, X - 1)], Q1)
    g_row = jnp.concatenate([grow[b] for b in range(X)], axis=1)
    u_pos = lax.broadcasted_iota(jnp.int32, (D, L), 1)
    t_off = lax.broadcasted_iota(jnp.int32, (D, L), 0)
    k1all = k1b[...].reshape(L, D)
    v1all = v1b[...].reshape(L, D)

    def inner(b, c):
        low = u_pos <= t_off + b * D
        gap = gcol[b] - g_row
        w = jnp.where(low, jnp.exp(jnp.where(low, gap, 0.0)), 0.0)
        wts[b] = w
        a = dot(q1b[b], k1all, NT) * w
        aw[b] = a
        raw[b] = dot_l(a, v1all, NN)
        return c

    lax.fori_loop(0, X, inner, 0)

    for j in range(3 * X):
        for ref, first in ((kdoc, (z - 2) * X), (qdoc, z * X)):
            at = first + j
            inside = (at >= 0) & (at < Z * X)
            value = docs[jnp.clip(at, 0, Z * X - 1)]
            ref[j] = jnp.full((1, D), jnp.where(inside, value, -1), jnp.int32)

    got(kall.at[pl.ds(X, X)], KA)
    put(kall.at[pl.ds(X + 1, X - 1)], kall.at[pl.ds(1, X - 1)], KB, zdev(1))
    got(qall.at[pl.ds(X, X)], QA)
    put(qall.at[pl.ds(X, X - 1)], qall.at[pl.ds(2 * X, X - 1)], QB, zdev(-1))

    def scan_local(backward, pieces, results):
        m = jnp.zeros((R, D), F32)
        for i in range(Z):
            at = Z - 1 - i if backward else i
            results[at] = m.astype(BF16)
            m = abuf[at] * m + pieces[at].astype(F32)

    got(sbuf.at[pl.ds(0, Z - 1)], SC1)
    got(abuf.at[pl.ds(0, Z - 1)], DEC)
    scan_local(False, sbuf, mst)
    scan_send(mst, mbuf, SC2)
    got(gall.at[pl.ds(X, X)], GA)
    put(gall.at[pl.ds(X, X - 1)], gall.at[pl.ds(2 * X, X - 1)], GB, zdev(-1))

    wide = lax.broadcasted_iota(jnp.int32, (D, W2), 1)
    tall = lax.broadcasted_iota(jnp.int32, (D, W2), 0)

    def window(ref, first):
        return ref[pl.ds(first, 2 * X)].reshape(W2, D)

    def window_row(ref, first):
        return jnp.concatenate([ref[first + i] for i in range(2 * X)], axis=1)

    got(kall.at[pl.ds(1, X - 1)], KB)

    def probs(b, c):
        s = dot(qall[b], window(kall, b + 1), NT) * scale
        ok = (window_row(kdoc, b + 1) == docs[z * X + b]) & (wide <= tall + (W2 - D))
        s = jnp.where(ok, s, FLOOR)
        peak = jnp.max(s, axis=1, keepdims=True)
        mass = jnp.sum(jnp.where(ok, jnp.exp(s - peak), 0.0), axis=1, keepdims=True)
        lse = peak + jnp.log(mass)
        pf[b] = jnp.where(ok, jnp.exp(s - lse), 0.0)
        lser[b] = to_row(lse)
        return c

    lax.fori_loop(0, X, probs, 0)
    put(lser, lsall.at[pl.ds(X, X)], LA, zdev(-1))
    put(lser, lsall.at[pl.ds(2 * X, X)], LB, zdev(-2))
    lsall[pl.ds(0, X)] = lser[...]

    got(qall.at[pl.ds(2 * X, X - 1)], QB)
    got(gall.at[pl.ds(2 * X, X - 1)], GB)
    got(lsall.at[pl.ds(X, X)], LA)
    got(lsall.at[pl.ds(2 * X, X)], LB)

    def probs_t(b, c):
        s = dot(kall[2 * X + b], window(qall, b), NT) * scale
        ok = (window_row(qdoc, b) == docs[z * X + b]) & (wide >= tall)
        p = jnp.where(ok, jnp.exp(jnp.where(ok, s - window_row(lsall, b), 0.0)), 0.0)
        pt[b] = p
        gv[b] = dot(p.astype(BF16), window(gall, b), NN)
        return c

    lax.fori_loop(0, X, probs_t, 0)

    got(mbuf.at[pl.ds(0, Z - 1)], SC2)
    m_state = mbuf[...].astype(F32).reshape(D, D).astype(BF16)

    def outer(b, c):
        r = raw[b] + jnp.exp(gcol[b]) * dot(q1b[b], m_state, NN)
        raw[b] = r
        pls[b] = to_row(jnp.sum(r * r, axis=1, keepdims=True))
        pls[X + b] = to_row(jnp.sum(r * gv[b], axis=1, keepdims=True))
        return c

    lax.fori_loop(0, X, outer, 0)

    def plane_send(i, c):
        put(pls, plb.at[i], PLN, pdev(i))
        return c

    lax.fori_loop(X * H // 2, X * H, plane_send, 0)
    lax.fori_loop(1, X * H // 2, plane_send, 0)
    plb[0] = pls[...]
    got(plb.at[pl.ds(1, X * H - 1)], PLN)
    sums = jnp.sum(plb[...], axis=0)
    inv_row = 1.0 / jnp.sqrt(sums[:X] / width_all + NORM_EPSILON)
    coef_row = inv_row * inv_row * inv_row * sums[X:] / width_all
    nrm[pl.ds(0, X)] = inv_row
    nrm[pl.ds(X, X)] = coef_row

    def finish(b, d_state):
        inv = to_col(nrm[b])
        coef = to_col(nrm[X + b])
        invc[b] = inv
        g = inv * gv[b] - raw[b] * coef
        rr[b] = g
        return d_state + dot(q1b[b], (g * jnp.exp(gcol[b])).astype(BF16), TN)

    d_state = lax.fori_loop(0, X, finish, jnp.zeros((D, D), F32))
    sst2[...] = d_state.reshape(Z, R, D).astype(BF16)
    scan_send(sst2, sbuf2, SC3)
    half = X // 2
    for b in range(X):
        vall[2 * X + b] = (raw[b] * invc[b]).astype(BF16)
    put(vall.at[pl.ds(2 * X + half, half)], vall.at[pl.ds(X + half, half)], VA, zdev(1))
    put(vall.at[pl.ds(2 * X, half)], vall.at[pl.ds(X, half)], VB, zdev(1))

    def give_back(n, out, phase):
        for d in range(1, X):
            put(ost.at[n, (x + d) % X], out.at[x], phase, xdev(d))
        out[x] = ost[n, x]


    def inner_q(b, c):
        g = rr[b].astype(BF16)
        back = (dot(g, v1all, NT) * wts[b]).astype(BF16)
        bw[b] = back
        rlow[b] = g
        part = dot(back, k1all, NN) + jnp.exp(gcol[b]) * dot(g, m_state, NT)
        ost[0, b] = part.astype(BF16)
        return c

    lax.fori_loop(0, X, inner_q, 0)
    got(vall.at[pl.ds(X + half, half)], VA)
    put(vall.at[pl.ds(X + half, half)], vall.at[pl.ds(half, half)], VC, zdev(1))
    give_back(0, o_q1, O0)
    q1all = q1b[...].reshape(L, D)
    rall = rlow[...].reshape(L, D)
    for b in range(X):
        own = pl.ds(b * D, D)
        ost[1, b] = dot(bw[:, :, own].reshape(L, D), q1all, TN).astype(BF16)
        ost[2, b] = dot(aw[:, :, own].reshape(L, D).astype(BF16), rall, TN).astype(BF16)
    got(vall.at[pl.ds(X, half)], VB)
    if half > 1:
        put(vall.at[pl.ds(X + 1, half - 1)], vall.at[pl.ds(1, half - 1)], VD, zdev(1))
    give_back(1, pk1, O1)
    give_back(2, pv1, O2)

    got(sbuf2.at[pl.ds(0, Z - 1)], SC3)
    scan_local(True, sbuf2, mst2)
    scan_send(mst2, mbuf2, SC4)

    got(vall.at[pl.ds(half, half)], VC)
    if half > 1:
        got(vall.at[pl.ds(1, half - 1)], VD)

    def query_grads(b, c):
        p = pf[b]
        gp = dot(gall[b], window(vall, b + 1), NT)
        delta = jnp.sum(p.astype(BF16).astype(F32) * gp, axis=1, keepdims=True)
        delr[b] = to_row(delta)
        ds = (p * (gp - delta) * scale).astype(BF16)
        ost[3, b] = dot(ds, window(kall, b + 1), NN).astype(BF16)
        return c

    lax.fori_loop(0, X, query_grads, 0)
    put(delr, dlall.at[pl.ds(X, X)], DA, zdev(-1))
    put(delr, dlall.at[pl.ds(2 * X, X)], DB, zdev(-2))
    dlall[pl.ds(0, X)] = delr[...]
    give_back(3, o_q2, O3)

    got(mbuf2.at[pl.ds(0, Z - 1)], SC4)
    lgs[...] = mbuf2[...].astype(F32).reshape(D, D).astype(BF16)
    for d in range(1, X):
        put(lgs, lgb.at[x], LG, xdev(d))
    lgb[x] = lgs[...]

    got(dlall.at[pl.ds(X, X)], DA)
    got(dlall.at[pl.ds(2 * X, X)], DB)

    def key_grads(b, c):
        gp = dot(vall[2 * X + b], window(gall, b), NT)
        ds = (pt[b] * (gp - window_row(dlall, b)) * scale).astype(BF16)
        ost[4, b] = dot(ds, window(qall, b), NN).astype(BF16)
        return c

    lax.fori_loop(0, X, key_grads, 0)
    give_back(4, o_k2, O4)

    got(pk1.at[pl.ds(0, X - 1)], O1)
    got(pv1.at[pl.ds(0, X - 1)], O2)
    got(tailb.at[pl.ds(0, X - 1)], TL)
    got(lgb.at[pl.ds(0, X - 1)], LG)

    def state_grads(h, c):
        tail = to_col(tailb[h])
        later = lgb[h]
        o_k1[h] = pk1[h].astype(F32) + tail * dot(hm[1, h], later, NT)
        o_v1[h] = pv1[h].astype(F32) + tail * dot(hm[0, h], later, NN)
        return c

    lax.fori_loop(0, X, state_grads, 0)

    for out, phase in ((o_q1, O0), (o_q2, O3), (o_k2, O4)):
        got(out.at[pl.ds(0, X - 1)], phase)
    for ref, phase in ((ldb, LD), (k1b, K1), (v1b, V1), (kall, K2), (qall, Q2), (gall, GO), (q1b, Q1),
                       (tailb, TL), (o_q1, O0), (pk1, O1), (pv1, O2), (o_q2, O3), (o_k2, O4), (lgb, LG)):
        sent(ref.at[pl.ds(0, X - 1)], phase)
    for ref, phase in ((sbuf, SC1), (abuf, DEC), (mbuf, SC2), (sbuf2, SC3), (mbuf2, SC4)):
        sent(ref.at[pl.ds(0, Z - 1)], phase)
    for ref, phase in ((kall, KA), (qall, QA), (gall, GA), (lser, LA), (lser, LB), (delr, DA), (delr, DB)):
        sent(ref.at[pl.ds(0, X)], phase)
    for ref, phase in ((kall, KB), (qall, QB), (gall, GB)):
        sent(ref.at[pl.ds(0, X - 1)], phase)
    for phase in (VA, VB, VC):
        sent(vall.at[pl.ds(0, half)], phase)
    if half > 1:
        sent(vall.at[pl.ds(0, half - 1)], VD)
    sent(plb.at[pl.ds(1, X * H - 1)], PLN)


def place(X, *refs):
    ins, outs, turned, store = refs[:5], refs[5:10], refs[10:15], refs[15]
    for n in range(5):
        for h in range(X):
            turned[n][:, h, :] = ins[n][h].astype(F32)
        pltpu.make_async_copy(turned[n], outs[n], store.at[n]).start()
    for n in range(5):
        pltpu.make_async_copy(turned[n], outs[n], store.at[n]).wait()


def make_body(Z, X, H):
    D = BLOCK

    def vm(*shape, dtype=F32):
        return pltpu.VMEM(shape, dtype)

    def body(q1, k1, v1, ld, q2, k2, go, docs):
        L = X * D
        low_blocks = jax.ShapeDtypeStruct((X, D, D), BF16)
        blocks = jax.ShapeDtypeStruct((X, D, D), F32)
        low = functools.partial(vm, dtype=BF16)
        scratch = [
            low(6, D, X, D), vm(D, X, D), low(6, X, D, D),
            low(X, D, D), low(X, D, D), low(X, D, D),
            low(3 * X, D, D), low(3 * X, D, D), low(3 * X, D, D), low(3 * X, D, D),
            vm(X, 1, D), vm(X, D, 1), vm(X, 1, D),
            vm(X, D, L), vm(X, D, L), vm(X, D, 2 * L), vm(X, D, 2 * L),
            vm(X, 1, D), vm(X, 1, D), vm(3 * X, 1, D), vm(3 * X, 1, D),
            vm(3 * X, 1, D, dtype=jnp.int32), vm(3 * X, 1, D, dtype=jnp.int32),
            low(Z, D // Z, D), low(Z, D // Z, D), low(Z, D // Z, D), low(Z, D // Z, D),
            low(Z, D // Z, D), low(Z, D // Z, D), low(Z, D // Z, D), low(Z, D // Z, D),
            vm(Z, 1, D), vm(1, D),
            vm(X, D, D), vm(X, D, D), vm(X, D, D),
            vm(2 * X, 1, D), vm(X * H, 2 * X, 1, D), vm(2 * X, 1, D),
            low(5, X, D, D), low(X, D, D), low(X, D, D),
            low(X, D, L), low(X, D, D), vm(X, D, D), vm(X, D, D),
            vm(X, 1, D), vm(X, 1, D), low(D, D), low(X, D, D),
            vm(X, 1, D), pltpu.SMEM((Z * X,), jnp.int32), vm(X, D, 1),
            pltpu.SemaphoreType.DMA((NSEM,)), pltpu.SemaphoreType.DMA((NSEM,)),
            pltpu.SemaphoreType.DMA((8,)),
        ]
        vmem = pl.BlockSpec(memory_space=pltpu.VMEM)
        hbm = pl.BlockSpec(memory_space=pltpu.HBM)
        outs = pl.pallas_call(
            functools.partial(kernel, Z, X, H, float(X * H * D)),
            out_shape=[low_blocks, blocks, blocks, low_blocks, low_blocks],
            in_specs=[hbm] * 8,
            out_specs=[vmem] * 5,
            scratch_shapes=scratch,
            compiler_params=pltpu.CompilerParams(
                collective_id=0, has_side_effects=True, vmem_limit_bytes=20 * 1024 * 1024),
        )(*[pltpu.with_memory_space_constraint(a, pltpu.HBM)
            for a in (q1, k1, v1, q2, k2, go, ld.reshape(X, 1, D), docs)])
        return tuple(pl.pallas_call(
            functools.partial(place, X),
            out_shape=[jax.ShapeDtypeStruct((D, X, D), F32)] * 5,
            in_specs=[vmem] * 5,
            out_specs=[hbm] * 5,
            scratch_shapes=[vm(D, X, D)] * 5 + [pltpu.SemaphoreType.DMA((5,))],
            compiler_params=pltpu.CompilerParams(vmem_limit_bytes=8 * 1024 * 1024),
        )(*outs))

    return body


def solution(mesh):
    split_both = P("seq", "head", None)
    placed = (split_both,) * 3 + (P("head", "seq"),) + (split_both,) * 3 + (P(),)
    return jax.shard_map(
        make_body(mesh.shape["seq"] // ROW, ROW, mesh.shape["head"]),
        mesh=mesh,
        in_specs=placed,
        out_specs=(split_both,) * 5,
        check_vma=False,
    )
```

```python
import functools
import math

import jax
import jax.numpy as jnp
from jax import lax
from jax.experimental import pallas as pl
from jax.experimental.pallas import tpu as pltpu
from jax.sharding import PartitionSpec as P

BLOCK = 128
ROW = 4
NORM_EPSILON = 1e-05
FLOOR = -1e30
MESH = pl.DeviceIdType.MESH
F32 = jnp.float32
BF16 = jnp.bfloat16

(LD, K1, V1, K2, Q2, GO, Q1, TL, SC1, DEC, SC2, KA, KB, QA, QB, GA, GB, LA, LB, PLN,
 SC3, SC4, VA, VB, VC, VD, DA, DB, O0, O1, O2, O3, O4, LG) = range(34)
NSEM = 34
NHELLO = 6

NN = (((1,), (0,)), ((), ()))
NT = (((1,), (1,)), ((), ()))
TN = (((0,), (0,)), ((), ()))


def dot(a, b, dims):
    return lax.dot_general(a, b, dims, preferred_element_type=F32)


def split(a):
    high = a.astype(BF16)
    return high, (a - high.astype(F32)).astype(BF16)


def dot_l(a, b, dims):
    high, low = split(a)
    return dot(high, b, dims) + dot(low, b, dims)


def dot_r(a, b, dims):
    high, low = split(b)
    return dot(a, high, dims) + dot(a, low, dims)


def kernel(Z, X, H, width_all, q1_in, k1_in, v1_in, q2_in, k2_in, go_in, ld_in, docs_in,
           o_q1, o_k1, o_v1, o_q2, o_k2,
           raw_in, wide_in, hm, q1b, k1b, v1b, kall, qall, gall, vall, ldb, gcol, grow,
           wts, aw, pf, pt, lser, delr, lsall, dlall, kdoc, qdoc,
           sst, sbuf, mst, mbuf, sst2, sbuf2, mst2, mbuf2, abuf, arow,
           raw, gv, rr, pls, plb, nrm, ost, pk1, pv1, bw, rlow, dk1, dv1,
           tails, tailb, lgs, lgb, ld, docs, invc, send, recv, load, hello):
    D = BLOCK
    L = X * BLOCK
    W2 = 2 * L
    R = D // Z
    me = lax.axis_index("seq")
    hd = lax.axis_index("head")
    z = me // X
    x = me % X
    scale = 1.0 / math.sqrt(D)
    half = X // 2

    def xdev(d):
        return (z * X + (x + d) % X, hd)

    def zdev(d):
        return (((z + d + Z) % Z) * X + x, hd)

    def pdev(i):
        return (z * X + (x + i // H) % X, (hd + i % H) % H)

    def each(blocks, work, carry=0):
        for b in blocks:
            carry = work(b, carry)
        return carry

    def put(src, dst, phase, dev):
        c = pltpu.make_async_remote_copy(
            src_ref=src, dst_ref=dst, send_sem=send.at[phase], recv_sem=recv.at[phase],
            device_id=dev, device_id_type=MESH)
        c.start()

    def got(ref, phase):
        pltpu.make_async_copy(ref, ref, recv.at[phase]).wait()

    def sent(ref, phase):
        pltpu.make_async_copy(ref, ref, send.at[phase]).wait()

    barrier = pltpu.get_barrier_semaphore()

    near = [xdev(d) for d in range(1, X)] + [zdev(1), zdev(-1)]
    same_x = [(me, (hd + d) % H) for d in range(1, H)]
    for dev in near + same_x:
        pl.semaphore_signal(barrier, inc=1, device_id=dev, device_id_type=MESH)

    def greet(number, devices):
        for dev in devices:
            pl.semaphore_signal(hello.at[number], inc=1, device_id=dev, device_id_type=MESH)

    sources = (k1_in, v1_in, k2_in, q2_in, go_in, q1_in)
    pltpu.make_async_copy(ld_in, ld, load.at[6]).start()
    for n, src in enumerate(sources):
        pltpu.make_async_copy(src, raw_in.at[n], load.at[n]).start()
    pltpu.make_async_copy(docs_in, docs, load.at[7]).start()

    def heads_first(n):
        pltpu.make_async_copy(sources[n], raw_in.at[n], load.at[n]).wait()
        wide_in[n % 2] = raw_in[n].astype(F32)
        for h in range(X):
            hm[n, h] = wide_in[n % 2, :, h, :].astype(BF16)

    def exchange(src, dst, base, phase):
        for d in range(1, X):
            put(src.at[(x + d) % X], dst.at[base + x], phase, xdev(d))
        dst[base + x] = src[x]

    pltpu.make_async_copy(ld_in, ld, load.at[6]).wait()
    heads_first(0)
    heads_first(1)
    pl.semaphore_wait(barrier, len(near) + len(same_x))
    exchange(ld, ldb, 0, LD)
    exchange(hm.at[0], k1b, 0, K1)
    exchange(hm.at[1], v1b, 0, V1)

    reach = 1
    greet(0, [zdev(reach), zdev(-reach)])
    greet(NHELLO - 1, same_x)
    heads_first(2)
    put(hm.at[2, x], kall.at[X + x], KA, zdev(1))
    exchange(hm.at[2], kall, 2 * X, K2)
    heads_first(3)
    put(hm.at[3, x], qall.at[X + x], QA, zdev(-1))
    exchange(hm.at[3], qall, 0, Q2)
    rounds = 0
    pl.semaphore_wait(hello.at[rounds], 2)
    reach, rounds = 2, 1
    if reach < Z // 2:
        greet(rounds, [zdev(reach), zdev(-reach)])
    heads_first(4)
    put(hm.at[4, x], gall.at[X + x], GA, zdev(-1))
    exchange(hm.at[4], gall, 0, GO)
    heads_first(5)
    exchange(hm.at[5], q1b, 0, Q1)
    pltpu.make_async_copy(docs_in, docs, load.at[7]).wait()
    pl.semaphore_wait(hello.at[NHELLO - 1], len(same_x))
    while reach < Z // 2:
        pl.semaphore_wait(hello.at[rounds], 2)
        reach, rounds = 2 * reach, rounds + 1
        if reach < Z // 2:
            greet(rounds, [zdev(reach), zdev(-reach)])
        if rounds == 2:
            break

    rows = lax.broadcasted_iota(jnp.int32, (D, D), 0)
    cols = lax.broadcasted_iota(jnp.int32, (D, D), 1)
    eye = rows == cols

    def to_row(col):
        return jnp.sum(jnp.where(eye, col, 0.0), axis=0, keepdims=True)

    def to_col(row):
        return jnp.sum(jnp.where(eye, row, 0.0), axis=1, keepdims=True)

    got(ldb.at[pl.ds(0, X - 1)], LD)
    offset = jnp.zeros((1, 1), F32)
    for b in range(X):
        row = ldb[b]
        col = jnp.sum(jnp.where(cols <= rows, row, 0.0), axis=1, keepdims=True) + offset
        gcol[b] = col
        grow[b] = to_row(col)
        offset = offset + jnp.sum(row, axis=1, keepdims=True)
    g_end = offset
    arow[...] = jnp.broadcast_to(jnp.exp(g_end), (1, D))
    for b in range(X):
        tails[b] = jnp.exp(g_end - grow[b])

    got(k1b.at[pl.ds(0, X - 1)], K1)
    got(v1b.at[pl.ds(0, X - 1)], V1)

    def add_state(b, s):
        vd = v1b[b].astype(F32) * jnp.exp(g_end - gcol[b])
        return s + dot_r(k1b[b], vd, TN)

    state = each(range(X), add_state, jnp.zeros((D, D), F32))
    sst[...] = state.reshape(Z, R, D).astype(BF16)
    while reach < Z // 2:
        pl.semaphore_wait(hello.at[rounds], 2)
        reach, rounds = 2 * reach, rounds + 1
        if reach < Z // 2:
            greet(rounds, [zdev(reach), zdev(-reach)])

    def far_first(i):
        return Z // 2 + ((i + 1) // 2) * (2 * (i % 2) - 1)

    def scan_send(src, dst, phase):
        def one(i, c):
            d = far_first(i)
            to = (z + d) % Z
            put(src.at[to], dst.at[z], phase, zdev(d))
            return c
        lax.fori_loop(0, Z - 1, one, 0)
        dst[z] = src[z]

    scan_send(sst, sbuf, SC1)

    def decay_send(i, c):
        put(arow, abuf.at[z], DEC, zdev(far_first(i)))
        return c

    lax.fori_loop(0, Z - 1, decay_send, 0)
    abuf[z] = arow[...]

    def pass_on(ref, base, phase, dev):
        for d in range(1, X):
            at = (x + d) % X
            put(ref.at[base + at], ref.at[X + at], phase, dev)

    got(kall.at[pl.ds(0, X - 1)], K2)
    pass_on(kall, 2 * X, KA, zdev(1))
    got(qall.at[pl.ds(0, X - 1)], Q2)
    pass_on(qall, 0, QA, zdev(-1))
    got(gall.at[pl.ds(0, X - 1)], GO)
    pass_on(gall, 0, GA, zdev(-1))
    exchange(tails, tailb, 0, TL)

    for j in range(3 * X):
        for ref, first in ((kdoc, (z - 2) * X), (qdoc, z * X)):
            at = first + j
            inside = (at >= 0) & (at < Z * X)
            value = docs[jnp.clip(at, 0, Z * X - 1)]
            ref[j] = jnp.full((1, D), jnp.where(inside, value, -1), jnp.int32)

    got(kall.at[pl.ds(X, X)], KA)
    put(kall.at[pl.ds(X + 1, X - 1)], kall.at[pl.ds(1, X - 1)], KB, zdev(1))
    got(q1b.at[pl.ds(0, X - 1)], Q1)
    g_row = jnp.concatenate([grow[b] for b in range(X)], axis=1)
    u_pos = lax.broadcasted_iota(jnp.int32, (D, L), 1)
    t_off = lax.broadcasted_iota(jnp.int32, (D, L), 0)
    k1all = k1b[...].reshape(L, D)
    v1all = v1b[...].reshape(L, D)

    def inner(b, c):
        low = u_pos <= t_off + b * D
        gap = gcol[b] - g_row
        w = jnp.where(low, jnp.exp(jnp.where(low, gap, 0.0)), 0.0)
        wts[b] = w
        a = dot(q1b[b], k1all, NT) * w
        aw[b] = a
        raw[b] = dot_l(a, v1all, NN)
        return c

    each(range(0, half), inner)
    got(qall.at[pl.ds(X, X)], QA)
    put(qall.at[pl.ds(X, X - 1)], qall.at[pl.ds(2 * X, X - 1)], QB, zdev(-1))

    def scan_local(backward, pieces, results):
        m = jnp.zeros((R, D), F32)
        for i in range(Z):
            at = Z - 1 - i if backward else i
            results[at] = m.astype(BF16)
            m = abuf[at] * m + pieces[at].astype(F32)

    got(sbuf.at[pl.ds(0, Z - 1)], SC1)
    got(abuf.at[pl.ds(0, Z - 1)], DEC)
    scan_local(False, sbuf, mst)
    scan_send(mst, mbuf, SC2)
    each(range(half, X), inner)
    got(gall.at[pl.ds(X, X)], GA)
    put(gall.at[pl.ds(X, X - 1)], gall.at[pl.ds(2 * X, X - 1)], GB, zdev(-1))

    wide = lax.broadcasted_iota(jnp.int32, (D, W2), 1)
    tall = lax.broadcasted_iota(jnp.int32, (D, W2), 0)

    def window(ref, first):
        return ref[pl.ds(first, 2 * X)].reshape(W2, D)

    def window_row(ref, first):
        return jnp.concatenate([ref[first + i] for i in range(2 * X)], axis=1)

    def probs(b, c):
        s = dot(qall[b], window(kall, b + 1), NT) * scale
        ok = (window_row(kdoc, b + 1) == docs[z * X + b]) & (wide <= tall + (W2 - D))
        s = jnp.where(ok, s, FLOOR)
        peak = jnp.max(s, axis=1, keepdims=True)
        mass = jnp.sum(jnp.where(ok, jnp.exp(s - peak), 0.0), axis=1, keepdims=True)
        lse = peak + jnp.log(mass)
        pf[b] = jnp.where(ok, jnp.exp(s - lse), 0.0)
        lser[b] = to_row(lse)
        return c

    probs(X - 1, 0)
    got(kall.at[pl.ds(1, X - 1)], KB)
    each(range(X - 1), probs)
    put(lser, lsall.at[pl.ds(X, X)], LA, zdev(-1))
    put(lser, lsall.at[pl.ds(2 * X, X)], LB, zdev(-2))
    lsall[pl.ds(0, X)] = lser[...]

    def probs_t(b, c):
        s = dot(kall[2 * X + b], window(qall, b), NT) * scale
        ok = (window_row(qdoc, b) == docs[z * X + b]) & (wide >= tall)
        p = jnp.where(ok, jnp.exp(jnp.where(ok, s - window_row(lsall, b), 0.0)), 0.0)
        pt[b] = p
        gv[b] = dot(p.astype(BF16), window(gall, b), NN)
        return c

    got(lsall.at[pl.ds(X, X)], LA)
    probs_t(0, 0)
    got(qall.at[pl.ds(2 * X, X - 1)], QB)
    got(gall.at[pl.ds(2 * X, X - 1)], GB)
    got(lsall.at[pl.ds(2 * X, X)], LB)
    each(range(1, X), probs_t)

    got(mbuf.at[pl.ds(0, Z - 1)], SC2)
    m_state = mbuf[...].astype(F32).reshape(D, D).astype(BF16)

    def outer(b, c):
        r = raw[b] + jnp.exp(gcol[b]) * dot(q1b[b], m_state, NN)
        raw[b] = r
        pls[pl.ds(b, 1), :] = to_row(jnp.sum(r * r, axis=1, keepdims=True))
        pls[pl.ds(X + b, 1), :] = to_row(jnp.sum(r * gv[b], axis=1, keepdims=True))
        return c

    each(range(X), outer)

    def plane_send(i, c):
        put(pls, plb.at[i], PLN, pdev(i))
        return c

    lax.fori_loop(X * H // 2, X * H, plane_send, 0)
    lax.fori_loop(1, X * H // 2, plane_send, 0)
    plb[0] = pls[...]
    got(plb.at[pl.ds(1, X * H - 1)], PLN)
    sums = jnp.sum(plb[...], axis=0)
    inv_row = 1.0 / jnp.sqrt(sums[:X] / width_all + NORM_EPSILON)
    coef_row = inv_row * inv_row * inv_row * sums[X:] / width_all
    nrm[pl.ds(0, X), :] = inv_row
    nrm[pl.ds(X, X), :] = coef_row

    def finish(b, d_state):
        inv = to_col(nrm[pl.ds(b, 1), :])
        coef = to_col(nrm[pl.ds(X + b, 1), :])
        invc[b] = inv
        g = inv * gv[b] - raw[b] * coef
        rr[b] = g
        return d_state + dot(q1b[b], (g * jnp.exp(gcol[b])).astype(BF16), TN)

    d_state = each(range(X), finish, jnp.zeros((D, D), F32))
    sst2[...] = d_state.reshape(Z, R, D).astype(BF16)
    scan_send(sst2, sbuf2, SC3)
    for b in range(X):
        vall[2 * X + b] = (raw[b] * invc[b]).astype(BF16)
    put(vall.at[pl.ds(2 * X + half, half)], vall.at[pl.ds(X + half, half)], VA, zdev(1))
    put(vall.at[pl.ds(2 * X, half)], vall.at[pl.ds(X, half)], VB, zdev(1))

    def give_back(n, out, phase):
        for d in range(1, X):
            put(ost.at[n, (x + d) % X], out.at[x], phase, xdev(d))
        out[x] = ost[n, x]


    def inner_q(b, c):
        g = rr[b].astype(BF16)
        back = (dot(g, v1all, NT) * wts[b]).astype(BF16)
        bw[b] = back
        rlow[b] = g
        part = dot(back, k1all, NN) + jnp.exp(gcol[b]) * dot(g, m_state, NT)
        ost[0, b] = part.astype(BF16)
        return c

    each(range(X), inner_q)
    got(vall.at[pl.ds(X + half, half)], VA)
    put(vall.at[pl.ds(X + half, half)], vall.at[pl.ds(half, half)], VC, zdev(1))
    give_back(0, o_q1, O0)
    q1all = q1b[...].reshape(L, D)
    rall = rlow[...].reshape(L, D)
    for b in range(X):
        own = pl.ds(b * D, D)
        ost[1, b] = dot(bw[:, :, own].reshape(L, D), q1all, TN).astype(BF16)
        ost[2, b] = dot(aw[:, :, own].reshape(L, D).astype(BF16), rall, TN).astype(BF16)
    got(vall.at[pl.ds(X, half)], VB)
    if half > 1:
        put(vall.at[pl.ds(X + 1, half - 1)], vall.at[pl.ds(1, half - 1)], VD, zdev(1))
    give_back(1, pk1, O1)
    give_back(2, pv1, O2)

    got(sbuf2.at[pl.ds(0, Z - 1)], SC3)
    scan_local(True, sbuf2, mst2)
    scan_send(mst2, mbuf2, SC4)

    def query_grads(b, c):
        p = pf[b]
        gp = dot(gall[b], window(vall, b + 1), NT)
        delta = jnp.sum(p.astype(BF16).astype(F32) * gp, axis=1, keepdims=True)
        delr[b] = to_row(delta)
        ds = (p * (gp - delta) * scale).astype(BF16)
        ost[3, b] = dot(ds, window(kall, b + 1), NN).astype(BF16)
        return c

    query_grads(X - 1, 0)
    got(vall.at[pl.ds(half, half)], VC)
    each(range(X - 2, half - 2, -1), query_grads)
    if half > 1:
        got(vall.at[pl.ds(1, half - 1)], VD)
        each(range(half - 2, -1, -1), query_grads)
    put(delr, dlall.at[pl.ds(X, X)], DA, zdev(-1))
    put(delr, dlall.at[pl.ds(2 * X, X)], DB, zdev(-2))
    dlall[pl.ds(0, X)] = delr[...]
    give_back(3, o_q2, O3)

    got(mbuf2.at[pl.ds(0, Z - 1)], SC4)
    lgs[...] = mbuf2[...].astype(F32).reshape(D, D).astype(BF16)
    for d in range(1, X):
        put(lgs, lgb.at[x], LG, xdev(d))
    lgb[x] = lgs[...]

    got(dlall.at[pl.ds(X, X)], DA)
    got(dlall.at[pl.ds(2 * X, X)], DB)

    def key_grads(i, c):
        b = (x + i) % X
        gp = dot(vall[2 * X + b], window(gall, b), NT)
        ds = (pt[b] * (gp - window_row(dlall, b)) * scale).astype(BF16)
        part = dot(ds, window(qall, b), NN).astype(BF16)
        if i < X:
            ost[4, b] = part
            put(ost.at[4, b], o_k2.at[x], O4, xdev(i))
        else:
            o_k2[x] = part
        return c

    each(range(1, X + 1), key_grads)

    got(pk1.at[pl.ds(0, X - 1)], O1)
    got(pv1.at[pl.ds(0, X - 1)], O2)
    got(tailb.at[pl.ds(0, X - 1)], TL)
    got(lgb.at[pl.ds(0, X - 1)], LG)

    def state_grads(h, c):
        tail = to_col(tailb[h])
        later = lgb[h]
        o_k1[h] = pk1[h].astype(F32) + tail * dot(hm[1, h], later, NT)
        o_v1[h] = pv1[h].astype(F32) + tail * dot(hm[0, h], later, NN)
        return c

    each(range(X), state_grads)

    for out, phase in ((o_q1, O0), (o_q2, O3), (o_k2, O4)):
        got(out.at[pl.ds(0, X - 1)], phase)
    for ref, phase in ((ldb, LD), (k1b, K1), (v1b, V1), (kall, K2), (qall, Q2), (gall, GO), (q1b, Q1),
                       (tailb, TL), (o_q1, O0), (pk1, O1), (pv1, O2), (o_q2, O3), (o_k2, O4), (lgb, LG)):
        sent(ref.at[pl.ds(0, X - 1)], phase)
    for ref, phase in ((sbuf, SC1), (abuf, DEC), (mbuf, SC2), (sbuf2, SC3), (mbuf2, SC4)):
        sent(ref.at[pl.ds(0, Z - 1)], phase)
    for ref, phase in ((kall, KA), (qall, QA), (gall, GA), (lser, LA), (lser, LB), (delr, DA), (delr, DB)):
        sent(ref.at[pl.ds(0, X)], phase)
    for ref, phase in ((kall, KB), (qall, QB), (gall, GB)):
        sent(ref.at[pl.ds(0, X - 1)], phase)
    for phase in (VA, VB, VC):
        sent(vall.at[pl.ds(0, half)], phase)
    if half > 1:
        sent(vall.at[pl.ds(0, half - 1)], VD)
    sent(plb.at[pl.ds(1, X * H - 1)], PLN)


def place(X, *refs):
    ins, outs, turned, store = refs[:5], refs[5:10], refs[10:15], refs[15]
    for n in range(5):
        for h in range(X):
            turned[n][:, h, :] = ins[n][h].astype(F32)
        pltpu.make_async_copy(turned[n], outs[n], store.at[n]).start()
    for n in range(5):
        pltpu.make_async_copy(turned[n], outs[n], store.at[n]).wait()


def make_body(Z, X, H):
    D = BLOCK

    def vm(*shape, dtype=F32):
        return pltpu.VMEM(shape, dtype)

    def body(q1, k1, v1, ld, q2, k2, go, docs):
        L = X * D
        low_blocks = jax.ShapeDtypeStruct((X, D, D), BF16)
        blocks = jax.ShapeDtypeStruct((X, D, D), F32)
        low = functools.partial(vm, dtype=BF16)
        scratch = [
            low(6, D, X, D), vm(2, D, X, D), low(6, X, D, D),
            low(X, D, D), low(X, D, D), low(X, D, D),
            low(3 * X, D, D), low(3 * X, D, D), low(3 * X, D, D), low(3 * X, D, D),
            vm(X, 1, D), vm(X, D, 1), vm(X, 1, D),
            vm(X, D, L), vm(X, D, L), vm(X, D, 2 * L), vm(X, D, 2 * L),
            vm(X, 1, D), vm(X, 1, D), vm(3 * X, 1, D), vm(3 * X, 1, D),
            vm(3 * X, 1, D, dtype=jnp.int32), vm(3 * X, 1, D, dtype=jnp.int32),
            low(Z, D // Z, D), low(Z, D // Z, D), low(Z, D // Z, D), low(Z, D // Z, D),
            low(Z, D // Z, D), low(Z, D // Z, D), low(Z, D // Z, D), low(Z, D // Z, D),
            vm(Z, 1, D), vm(1, D),
            vm(X, D, D), vm(X, D, D), vm(X, D, D),
            vm(2 * X, D), vm(X * H, 2 * X, D), vm(2 * X, D),
            low(5, X, D, D), low(X, D, D), low(X, D, D),
            low(X, D, L), low(X, D, D), vm(X, D, D), vm(X, D, D),
            vm(X, 1, D), vm(X, 1, D), low(D, D), low(X, D, D),
            vm(X, 1, D), pltpu.SMEM((Z * X,), jnp.int32), vm(X, D, 1),
            pltpu.SemaphoreType.DMA((NSEM,)), pltpu.SemaphoreType.DMA((NSEM,)),
            pltpu.SemaphoreType.DMA((8,)), pltpu.SemaphoreType.REGULAR((NHELLO,)),
        ]
        vmem = pl.BlockSpec(memory_space=pltpu.VMEM)
        hbm = pl.BlockSpec(memory_space=pltpu.HBM)
        outs = pl.pallas_call(
            functools.partial(kernel, Z, X, H, float(X * H * D)),
            out_shape=[low_blocks, blocks, blocks, low_blocks, low_blocks],
            in_specs=[hbm] * 8,
            out_specs=[vmem] * 5,
            scratch_shapes=scratch,
            compiler_params=pltpu.CompilerParams(
                collective_id=0, has_side_effects=True, vmem_limit_bytes=20 * 1024 * 1024),
        )(*[pltpu.with_memory_space_constraint(a, pltpu.HBM)
            for a in (q1, k1, v1, q2, k2, go, ld.reshape(X, 1, D), docs)])
        return tuple(pl.pallas_call(
            functools.partial(place, X),
            out_shape=[jax.ShapeDtypeStruct((D, X, D), F32)] * 5,
            in_specs=[vmem] * 5,
            out_specs=[hbm] * 5,
            scratch_shapes=[vm(D, X, D)] * 5 + [pltpu.SemaphoreType.DMA((5,))],
            compiler_params=pltpu.CompilerParams(vmem_limit_bytes=8 * 1024 * 1024),
        )(*outs))

    return body


def solution(mesh):
    split_both = P("seq", "head", None)
    placed = (split_both,) * 3 + (P("head", "seq"),) + (split_both,) * 3 + (P(),)
    return jax.shard_map(
        make_body(mesh.shape["seq"] // ROW, ROW, mesh.shape["head"]),
        mesh=mesh,
        in_specs=placed,
        out_specs=(split_both,) * 5,
        check_vma=False,
    )
```

```python
import functools
import math

import jax
import jax.numpy as jnp
from jax import lax
from jax.experimental import pallas as pl
from jax.experimental.pallas import tpu as pltpu
from jax.sharding import PartitionSpec as P

BLOCK = 128
ROW = 4
NORM_EPSILON = 1e-05
FLOOR = -1e30
MESH = pl.DeviceIdType.MESH
F32 = jnp.float32
BF16 = jnp.bfloat16

(LD, K1, V1, Q1, TL, SC1, DEC, SC2, KA, KB, QA, QB, GA, GB, LA, LB, PLN,
 SC3, SC4, VA, VB, VC, VD, DA, DB, O0, O1, O2, O3, O4, LG, SP) = range(32)
K2, Q2, GO = 32, 35, 38
NSEM = 41
NHELLO = 3
NEAR = {16: (1, -1, 2, -2), 4: (1, -1, 2)}
AROUND = {4: (1, 3, 2), 2: (1,)}
FAR = {16: (2, 4), 4: ()}

NN = (((1,), (0,)), ((), ()))
NT = (((1,), (1,)), ((), ()))
TN = (((0,), (0,)), ((), ()))


def dot(a, b, dims):
    return lax.dot_general(a, b, dims, preferred_element_type=F32)


def split(a):
    high = a.astype(BF16)
    return high, (a - high.astype(F32)).astype(BF16)


def dot_l(a, b, dims):
    high, low = split(a)
    return dot(high, b, dims) + dot(low, b, dims)


def dot_r(a, b, dims):
    high, low = split(b)
    return dot(a, high, dims) + dot(a, low, dims)


def kernel(Z, X, H, width_all, q1_in, k1_in, v1_in, q2_in, k2_in, go_in, ld_in, docs_in,
           o_q1, o_k1, o_v1, o_q2, o_k2,
           raw_in, wide_in, hm, q1b, k1b, v1b, kall, qall, gall, vall, ldb, gcol, grow,
           wts, aw, pf, pt, lser, delr, lsall, dlall, kdoc, qdoc,
           sst, sbuf, mst, mbuf, sst2, sbuf2, mst2, mbuf2, abuf, arow,
           raw, gv, rr, pls, plb, nrm, ost, pk1, pv1, bw, rlow, dk1, dv1,
           tails, tailb, lgs, lgb, ld, docs, invc, spart, sblk, rq1, rq2, rk2, send, recv, load, hello):
    D = BLOCK
    L = X * BLOCK
    W2 = 2 * L
    R = D // Z
    me = lax.axis_index("seq")
    hd = lax.axis_index("head")
    z = me // X
    x = me % X
    scale = 1.0 / math.sqrt(D)
    half = X // 2

    def xdev(d):
        return (z * X + (x + d) % X, hd)

    def zdev(d):
        return (((z + d + Z) % Z) * X + x, hd)

    def pdev(i):
        return (z * X + (x + i // H) % X, (hd + i % H) % H)

    def each(blocks, work, carry=0):
        for b in blocks:
            carry = work(b, carry)
        return carry

    def put(src, dst, phase, dev):
        c = pltpu.make_async_remote_copy(
            src_ref=src, dst_ref=dst, send_sem=send.at[phase], recv_sem=recv.at[phase],
            device_id=dev, device_id_type=MESH)
        c.start()

    def got(ref, phase):
        pltpu.make_async_copy(ref, ref, recv.at[phase]).wait()

    def sent(ref, phase):
        pltpu.make_async_copy(ref, ref, send.at[phase]).wait()

    barrier = pltpu.get_barrier_semaphore()
    sources = (k1_in, v1_in, k2_in, q2_in, go_in, q1_in)
    near = [zdev(d) for d in NEAR[Z]] + [xdev(d) for d in range(1, X)]
    same_x = [(me, (hd + d) % H) for d in range(1, H)]
    for dev in near:
        pl.semaphore_signal(barrier, inc=1, device_id=dev, device_id_type=MESH)
    pltpu.make_async_copy(ld_in, ld, load.at[6]).start()
    for n, src in enumerate(sources):
        pltpu.make_async_copy(src, raw_in.at[n], load.at[n]).start()
    pltpu.make_async_copy(docs_in, docs, load.at[7]).start()
    for dev in same_x:
        pl.semaphore_signal(barrier, inc=1, device_id=dev, device_id_type=MESH)

    def greet(number, devices):
        for dev in devices:
            pl.semaphore_signal(hello.at[number], inc=1, device_id=dev, device_id_type=MESH)

    rows = lax.broadcasted_iota(jnp.int32, (D, D), 0)
    cols = lax.broadcasted_iota(jnp.int32, (D, D), 1)
    eye = rows == cols

    def to_row(col):
        return jnp.sum(jnp.where(eye, col, 0.0), axis=0, keepdims=True)

    def to_col(row):
        return jnp.sum(jnp.where(eye, row, 0.0), axis=1, keepdims=True)

    def heads_first(n):
        pltpu.make_async_copy(sources[n], raw_in.at[n], load.at[n]).wait()
        wide_in[n % 2] = raw_in[n].astype(F32)
        for h in range(X):
            hm[n, h] = wide_in[n % 2, :, h, :].astype(BF16)

    def exchange(src, dst, base, phase, apart=False):
        for d in AROUND[X]:
            put(src.at[(x + d) % X], dst.at[base + x], phase + (d - 1) * apart, xdev(d))
        dst[base + x] = src[x]

    pltpu.make_async_copy(ld_in, ld, load.at[6]).wait()
    heads_first(0)
    heads_first(1)
    for h in range(X):
        row = ld[h]
        col = jnp.sum(jnp.where(cols <= rows, row, 0.0), axis=1, keepdims=True)
        left = jnp.exp(jnp.sum(row, axis=1, keepdims=True) - col)
        spart[h] = dot_r(hm[0, h], hm[1, h].astype(F32) * left, TN).astype(BF16)
    pl.semaphore_wait(barrier, len(near) + len(same_x))
    greet(0, same_x)
    for number, reach in enumerate(FAR[Z]):
        if number == 0:
            greet(1, [zdev(reach), zdev(-reach)])

    exchange(ld, ldb, 0, LD)
    exchange(spart, sblk, 0, SP)
    heads_first(2)
    exchange(hm.at[2], kall, 2 * X, K2, True)
    heads_first(3)
    exchange(hm.at[3], qall, 0, Q2, True)
    for number, reach in enumerate(FAR[Z]):
        if number == 1:
            pl.semaphore_wait(hello.at[number], 2)
            greet(number + 1, [zdev(reach), zdev(-reach)])
    heads_first(4)
    exchange(hm.at[4], gall, 0, GO, True)
    exchange(hm.at[0], k1b, 0, K1)
    exchange(hm.at[1], v1b, 0, V1)
    heads_first(5)
    exchange(hm.at[5], q1b, 0, Q1)
    put(hm.at[2, x], kall.at[X + x], KA, zdev(1))
    put(hm.at[3, x], qall.at[X + x], QA, zdev(-1))
    put(hm.at[4, x], gall.at[X + x], GA, zdev(-1))
    pltpu.make_async_copy(docs_in, docs, load.at[7]).wait()
    pl.semaphore_wait(hello.at[0], len(same_x))

    got(ldb.at[pl.ds(0, X - 1)], LD)
    offset = jnp.zeros((1, 1), F32)
    ends = []
    for b in range(X):
        row = ldb[b]
        col = jnp.sum(jnp.where(cols <= rows, row, 0.0), axis=1, keepdims=True) + offset
        gcol[b] = col
        grow[b] = to_row(col)
        offset = offset + jnp.sum(row, axis=1, keepdims=True)
        ends.append(offset)
    g_end = offset
    arow[...] = jnp.broadcast_to(jnp.exp(g_end), (1, D))
    for b in range(X):
        tails[b] = jnp.exp(g_end - grow[b])

    got(sblk.at[pl.ds(0, X - 1)], SP)
    state = jnp.zeros((D, D), F32)
    for b in range(X):
        state = state + jnp.exp(g_end - ends[b]) * sblk[b].astype(F32)
    sst[...] = state.reshape(Z, R, D).astype(BF16)
    if FAR[Z]:
        pl.semaphore_wait(hello.at[len(FAR[Z])], 2)

    def far_first(i):
        return Z // 2 + ((i + 1) // 2) * (2 * (i % 2) - 1)

    def scan_send(src, dst, phase, decays=False):
        def one(i, c):
            d = far_first(i)
            to = (z + d) % Z
            if decays:
                put(arow, abuf.at[z], DEC, zdev(d))
            put(src.at[to], dst.at[z], phase, zdev(d))
            return c
        lax.fori_loop(0, Z - 1, one, 0)
        dst[z] = src[z]

    abuf[z] = arow[...]
    scan_send(sst, sbuf, SC1, True)

    def pass_on(ref, base, come, phase, dev):
        for d in AROUND[X]:
            at = (x - d + X) % X
            got(ref.at[pl.ds(0, 1)], come + d - 1)
            put(ref.at[base + at], ref.at[X + at], phase, dev)

    pass_on(kall, 2 * X, K2, KA, zdev(1))
    pass_on(qall, 0, Q2, QA, zdev(-1))
    pass_on(gall, 0, GO, GA, zdev(-1))

    for j in range(3 * X):
        for ref, first in ((kdoc, (z - 2) * X), (qdoc, z * X)):
            at = first + j
            inside = (at >= 0) & (at < Z * X)
            value = docs[jnp.clip(at, 0, Z * X - 1)]
            ref[j] = jnp.full((1, D), jnp.where(inside, value, -1), jnp.int32)

    got(kall.at[pl.ds(X, X)], KA)
    put(kall.at[pl.ds(X + 1, X - 1)], kall.at[pl.ds(1, X - 1)], KB, zdev(1))
    got(qall.at[pl.ds(X, X)], QA)
    put(qall.at[pl.ds(X, X - 1)], qall.at[pl.ds(2 * X, X - 1)], QB, zdev(-1))
    exchange(tails, tailb, 0, TL)
    got(k1b.at[pl.ds(0, X - 1)], K1)
    got(v1b.at[pl.ds(0, X - 1)], V1)
    got(q1b.at[pl.ds(0, X - 1)], Q1)
    g_row = jnp.concatenate([grow[b] for b in range(X)], axis=1)
    u_pos = lax.broadcasted_iota(jnp.int32, (D, L), 1)
    t_off = lax.broadcasted_iota(jnp.int32, (D, L), 0)
    k1all = k1b[...].reshape(L, D)
    v1all = v1b[...].reshape(L, D)

    def inner(b, c):
        low = u_pos <= t_off + b * D
        gap = gcol[b] - g_row
        w = jnp.where(low, jnp.exp(jnp.where(low, gap, 0.0)), 0.0)
        wts[b] = w
        a = dot(q1b[b], k1all, NT) * w
        aw[b] = a
        raw[b] = dot_l(a, v1all, NN)
        return c

    each(range(0, half), inner)
    def scan_local(backward, pieces, results):
        m = jnp.zeros((R, D), F32)
        for i in range(Z):
            at = Z - 1 - i if backward else i
            results[at] = m.astype(BF16)
            m = abuf[at] * m + pieces[at].astype(F32)

    got(sbuf.at[pl.ds(0, Z - 1)], SC1)
    got(abuf.at[pl.ds(0, Z - 1)], DEC)
    scan_local(False, sbuf, mst)
    scan_send(mst, mbuf, SC2)
    got(gall.at[pl.ds(X, X)], GA)
    put(gall.at[pl.ds(X, X - 1)], gall.at[pl.ds(2 * X, X - 1)], GB, zdev(-1))

    wide = lax.broadcasted_iota(jnp.int32, (D, W2), 1)
    tall = lax.broadcasted_iota(jnp.int32, (D, W2), 0)

    def window(ref, first):
        return ref[pl.ds(first, 2 * X)].reshape(W2, D)

    def window_row(ref, first):
        return jnp.concatenate([ref[first + i] for i in range(2 * X)], axis=1)

    def probs(b, c):
        s = dot(qall[b], window(kall, b + 1), NT) * scale
        ok = (window_row(kdoc, b + 1) == docs[z * X + b]) & (wide <= tall + (W2 - D))
        s = jnp.where(ok, s, FLOOR)
        peak = jnp.max(s, axis=1, keepdims=True)
        mass = jnp.sum(jnp.where(ok, jnp.exp(s - peak), 0.0), axis=1, keepdims=True)
        lse = peak + jnp.log(mass)
        pf[b] = jnp.where(ok, jnp.exp(s - lse), 0.0)
        lser[b] = to_row(lse)
        return c

    probs(X - 1, 0)
    got(kall.at[pl.ds(1, X - 1)], KB)
    each(range(X - 1), probs)
    put(lser, lsall.at[pl.ds(X, X)], LA, zdev(-1))
    put(lser, lsall.at[pl.ds(2 * X, X)], LB, zdev(-2))
    lsall[pl.ds(0, X)] = lser[...]
    each(range(half, X), inner)

    def probs_t(b, c):
        s = dot(kall[2 * X + b], window(qall, b), NT) * scale
        ok = (window_row(qdoc, b) == docs[z * X + b]) & (wide >= tall)
        p = jnp.where(ok, jnp.exp(jnp.where(ok, s - window_row(lsall, b), 0.0)), 0.0)
        pt[b] = p
        gv[b] = dot(p.astype(BF16), window(gall, b), NN)
        return c

    got(lsall.at[pl.ds(X, X)], LA)
    probs_t(0, 0)
    got(qall.at[pl.ds(2 * X, X - 1)], QB)
    got(gall.at[pl.ds(2 * X, X - 1)], GB)
    got(lsall.at[pl.ds(2 * X, X)], LB)
    each(range(1, X), probs_t)

    got(mbuf.at[pl.ds(0, Z - 1)], SC2)
    m_state = mbuf[...].astype(F32).reshape(D, D).astype(BF16)

    def outer(b, c):
        r = raw[b] + jnp.exp(gcol[b]) * dot(q1b[b], m_state, NN)
        raw[b] = r
        pls[pl.ds(b, 1), :] = to_row(jnp.sum(r * r, axis=1, keepdims=True))
        pls[pl.ds(X + b, 1), :] = to_row(jnp.sum(r * gv[b], axis=1, keepdims=True))
        return c

    each(range(X), outer)

    def plane_send(i, c):
        put(pls, plb.at[i], PLN, pdev(i))
        return c

    lax.fori_loop(X * H // 2, X * H, plane_send, 0)
    lax.fori_loop(1, X * H // 2, plane_send, 0)
    plb[0] = pls[...]
    got(plb.at[pl.ds(1, X * H - 1)], PLN)
    sums = jnp.sum(plb[...], axis=0)
    inv_row = 1.0 / jnp.sqrt(sums[:X] / width_all + NORM_EPSILON)
    coef_row = inv_row * inv_row * inv_row * sums[X:] / width_all
    nrm[pl.ds(0, X), :] = inv_row
    nrm[pl.ds(X, X), :] = coef_row

    def finish(b, d_state):
        inv = to_col(nrm[pl.ds(b, 1), :])
        coef = to_col(nrm[pl.ds(X + b, 1), :])
        invc[b] = inv
        g = inv * gv[b] - raw[b] * coef
        rr[b] = g
        return d_state + dot(q1b[b], (g * jnp.exp(gcol[b])).astype(BF16), TN)

    d_state = each(range(X), finish, jnp.zeros((D, D), F32))
    sst2[...] = d_state.reshape(Z, R, D).astype(BF16)
    scan_send(sst2, sbuf2, SC3)
    for b in range(X):
        vall[2 * X + b] = (raw[b] * invc[b]).astype(BF16)
    put(vall.at[pl.ds(2 * X + half, half)], vall.at[pl.ds(X + half, half)], VA, zdev(1))
    put(vall.at[pl.ds(2 * X, half)], vall.at[pl.ds(X, half)], VB, zdev(1))

    def give_back(n, out, phase):
        for d in range(1, X):
            put(ost.at[n, (x + d) % X], out.at[x], phase, xdev(d))
        out[x] = ost[n, x]


    def inner_q(b, c):
        g = rr[b].astype(BF16)
        back = (dot(g, v1all, NT) * wts[b]).astype(BF16)
        bw[b] = back
        rlow[b] = g
        part = dot(back, k1all, NN) + jnp.exp(gcol[b]) * dot(g, m_state, NT)
        ost[0, b] = part.astype(BF16)
        return c

    each(range(X), inner_q)
    got(vall.at[pl.ds(X + half, half)], VA)
    put(vall.at[pl.ds(X + half, half)], vall.at[pl.ds(half, half)], VC, zdev(1))
    give_back(0, rq1, O0)
    q1all = q1b[...].reshape(L, D)
    rall = rlow[...].reshape(L, D)
    for b in range(X):
        own = pl.ds(b * D, D)
        ost[1, b] = dot(bw[:, :, own].reshape(L, D), q1all, TN).astype(BF16)
        ost[2, b] = dot(aw[:, :, own].reshape(L, D).astype(BF16), rall, TN).astype(BF16)
    got(vall.at[pl.ds(X, half)], VB)
    if half > 1:
        put(vall.at[pl.ds(X + 1, half - 1)], vall.at[pl.ds(1, half - 1)], VD, zdev(1))
    give_back(1, pk1, O1)
    give_back(2, pv1, O2)

    got(sbuf2.at[pl.ds(0, Z - 1)], SC3)
    scan_local(True, sbuf2, mst2)
    scan_send(mst2, mbuf2, SC4)

    def query_grads(b, c):
        p = pf[b]
        gp = dot(gall[b], window(vall, b + 1), NT)
        delta = jnp.sum(p.astype(BF16).astype(F32) * gp, axis=1, keepdims=True)
        delr[b] = to_row(delta)
        ds = (p * (gp - delta) * scale).astype(BF16)
        ost[3, b] = dot(ds, window(kall, b + 1), NN).astype(BF16)
        return c

    query_grads(X - 1, 0)
    got(vall.at[pl.ds(half, half)], VC)
    each(range(X - 2, half - 2, -1), query_grads)
    if half > 1:
        got(vall.at[pl.ds(1, half - 1)], VD)
        each(range(half - 2, -1, -1), query_grads)
    put(delr, dlall.at[pl.ds(X, X)], DA, zdev(-1))
    put(delr, dlall.at[pl.ds(2 * X, X)], DB, zdev(-2))
    dlall[pl.ds(0, X)] = delr[...]
    give_back(3, rq2, O3)

    got(dlall.at[pl.ds(X, X)], DA)
    got(dlall.at[pl.ds(2 * X, X)], DB)

    def key_grads(i, c):
        b = (x + i) % X
        gp = dot(vall[2 * X + b], window(gall, b), NT)
        ds = (pt[b] * (gp - window_row(dlall, b)) * scale).astype(BF16)
        part = dot(ds, window(qall, b), NN).astype(BF16)
        if i < X:
            ost[4, b] = part
            put(ost.at[4, b], rk2.at[x], O4, xdev(i))
        else:
            rk2[x] = part
        return c

    each(range(1, half + 1), key_grads)

    got(mbuf2.at[pl.ds(0, Z - 1)], SC4)
    lgs[...] = mbuf2[...].astype(F32).reshape(D, D).astype(BF16)
    for d in range(1, X):
        put(lgs, lgb.at[x], LG, xdev(d))
    lgb[x] = lgs[...]
    each(range(half + 1, X + 1), key_grads)

    got(pk1.at[pl.ds(0, X - 1)], O1)
    got(pv1.at[pl.ds(0, X - 1)], O2)
    got(tailb.at[pl.ds(0, X - 1)], TL)

    def result(out, held, phase):
        got(held.at[pl.ds(0, X - 1)], phase)
        for h in range(X):
            out[:, h, :] = held[h].astype(F32)

    result(o_q1, rq1, O0)
    result(o_q2, rq2, O3)
    got(lgb.at[pl.ds(0, X - 1)], LG)

    def state_grads(h, c):
        tail = to_col(tailb[h])
        later = lgb[h]
        o_k1[:, h, :] = pk1[h].astype(F32) + tail * dot(hm[1, h], later, NT)
        o_v1[:, h, :] = pv1[h].astype(F32) + tail * dot(hm[0, h], later, NN)
        return c

    each(range(X), state_grads)

    result(o_k2, rk2, O4)
    for ref, phase in ((ldb, LD), (k1b, K1), (v1b, V1), (q1b, Q1),
                       (tailb, TL), (rq1, O0), (pk1, O1), (pv1, O2), (rq2, O3), (rk2, O4), (lgb, LG), (sblk, SP)):
        sent(ref.at[pl.ds(0, X - 1)], phase)
    for phase in (K2, Q2, GO):
        for d in range(1, X):
            sent(kall.at[pl.ds(0, 1)], phase + d - 1)
    for ref, phase in ((sbuf, SC1), (abuf, DEC), (mbuf, SC2), (sbuf2, SC3), (mbuf2, SC4)):
        sent(ref.at[pl.ds(0, Z - 1)], phase)
    for ref, phase in ((kall, KA), (qall, QA), (gall, GA), (lser, LA), (lser, LB), (delr, DA), (delr, DB)):
        sent(ref.at[pl.ds(0, X)], phase)
    for ref, phase in ((kall, KB), (qall, QB), (gall, GB)):
        sent(ref.at[pl.ds(0, X - 1)], phase)
    for phase in (VA, VB, VC):
        sent(vall.at[pl.ds(0, half)], phase)
    if half > 1:
        sent(vall.at[pl.ds(0, half - 1)], VD)
    sent(plb.at[pl.ds(1, X * H - 1)], PLN)


def place(*refs):
    ins, outs, store = refs[:5], refs[5:10], refs[10]
    for n in range(5):
        pltpu.make_async_copy(ins[n], outs[n], store.at[n]).start()
    for n in range(5):
        pltpu.make_async_copy(ins[n], outs[n], store.at[n]).wait()


def make_body(Z, X, H):
    D = BLOCK

    def vm(*shape, dtype=F32):
        return pltpu.VMEM(shape, dtype)

    def body(q1, k1, v1, ld, q2, k2, go, docs):
        L = X * D
        results = [jax.ShapeDtypeStruct((D, X, D), F32)] * 5
        low = functools.partial(vm, dtype=BF16)
        scratch = [
            low(6, D, X, D), vm(2, D, X, D), low(6, X, D, D),
            low(X, D, D), low(X, D, D), low(X, D, D),
            low(3 * X, D, D), low(3 * X, D, D), low(3 * X, D, D), low(3 * X, D, D),
            vm(X, 1, D), vm(X, D, 1), vm(X, 1, D),
            vm(X, D, L), vm(X, D, L), vm(X, D, 2 * L), vm(X, D, 2 * L),
            vm(X, 1, D), vm(X, 1, D), vm(3 * X, 1, D), vm(3 * X, 1, D),
            vm(3 * X, 1, D, dtype=jnp.int32), vm(3 * X, 1, D, dtype=jnp.int32),
            low(Z, D // Z, D), low(Z, D // Z, D), low(Z, D // Z, D), low(Z, D // Z, D),
            low(Z, D // Z, D), low(Z, D // Z, D), low(Z, D // Z, D), low(Z, D // Z, D),
            vm(Z, 1, D), vm(1, D),
            vm(X, D, D), vm(X, D, D), vm(X, D, D),
            vm(2 * X, D), vm(X * H, 2 * X, D), vm(2 * X, D),
            low(5, X, D, D), low(X, D, D), low(X, D, D),
            low(X, D, L), low(X, D, D), vm(X, D, D), vm(X, D, D),
            vm(X, 1, D), vm(X, 1, D), low(D, D), low(X, D, D),
            vm(X, 1, D), pltpu.SMEM((Z * X,), jnp.int32), vm(X, D, 1),
            low(X, D, D), low(X, D, D), low(X, D, D), low(X, D, D), low(X, D, D),
            pltpu.SemaphoreType.DMA((NSEM,)), pltpu.SemaphoreType.DMA((NSEM,)),
            pltpu.SemaphoreType.DMA((8,)), pltpu.SemaphoreType.REGULAR((NHELLO,)),
        ]
        vmem = pl.BlockSpec(memory_space=pltpu.VMEM)
        hbm = pl.BlockSpec(memory_space=pltpu.HBM)
        outs = pl.pallas_call(
            functools.partial(kernel, Z, X, H, float(X * H * D)),
            out_shape=results,
            in_specs=[hbm] * 8,
            out_specs=[vmem] * 5,
            scratch_shapes=scratch,
            compiler_params=pltpu.CompilerParams(
                collective_id=0, has_side_effects=True, vmem_limit_bytes=20 * 1024 * 1024),
        )(*[pltpu.with_memory_space_constraint(a, pltpu.HBM)
            for a in (q1, k1, v1, q2, k2, go, ld.reshape(X, 1, D), docs)])
        return tuple(pl.pallas_call(
            place,
            out_shape=results,
            in_specs=[vmem] * 5,
            out_specs=[hbm] * 5,
            scratch_shapes=[pltpu.SemaphoreType.DMA((5,))],
            compiler_params=pltpu.CompilerParams(vmem_limit_bytes=8 * 1024 * 1024),
        )(*outs))

    return body


def solution(mesh):
    split_both = P("seq", "head", None)
    placed = (split_both,) * 3 + (P("head", "seq"),) + (split_both,) * 3 + (P(),)
    return jax.shard_map(
        make_body(mesh.shape["seq"] // ROW, ROW, mesh.shape["head"]),
        mesh=mesh,
        in_specs=placed,
        out_specs=(split_both,) * 5,
        check_vma=False,
    )
```

```python
import functools
import math

import jax
import jax.numpy as jnp
from jax import lax
from jax.experimental import pallas as pl
from jax.experimental.pallas import tpu as pltpu
from jax.sharding import PartitionSpec as P

BLOCK = 128
ROW = 4
NORM_EPSILON = 1e-05
FLOOR = -1e30
MESH = pl.DeviceIdType.MESH
F32 = jnp.float32
BF16 = jnp.bfloat16

(LD, K1, V1, Q1, TL, SC1, DEC, SC2, KA, KB, QA, QB, GA, GB, LA, LB, PLN,
 SC3, SC4, VA, VB, VC, VD, DA, DB, O0, O1, O2, O3, O4, LG, SP) = range(32)
K2, Q2, GO = 32, 35, 38
NSEM = 41
NHELLO = 3
NEAR = {16: (1, -1, 2, -2), 4: (1, -1, 2)}
AROUND = {4: (1, 3, 2), 2: (1,)}
FARTHEST = {4: (2, 1, 3), 2: (1,)}
FAR = {16: (2, 4), 4: ()}

NN = (((1,), (0,)), ((), ()))
NT = (((1,), (1,)), ((), ()))
TN = (((0,), (0,)), ((), ()))


def dot(a, b, dims):
    return lax.dot_general(a, b, dims, preferred_element_type=F32)


def split(a):
    high = a.astype(BF16)
    return high, (a - high.astype(F32)).astype(BF16)


def dot_l(a, b, dims):
    high, low = split(a)
    return dot(high, b, dims) + dot(low, b, dims)


def dot_r(a, b, dims):
    high, low = split(b)
    return dot(a, high, dims) + dot(a, low, dims)


def kernel(Z, X, H, width_all, q1_in, k1_in, v1_in, q2_in, k2_in, go_in, ld_in, docs_in,
           o_q1, o_k1, o_v1, o_q2, o_k2,
           raw_in, wide_in, hm, q1b, k1b, v1b, kall, qall, gall, vall, ldb, gcol, grow,
           wts, aw, pf, pt, lser, delr, lsall, dlall, kdoc, qdoc,
           sst, sbuf, mst, mbuf, sst2, sbuf2, mst2, mbuf2, abuf, arow,
           raw, gv, rr, pls, plb, nrm, ost, pk1, pv1, bw, rlow, dk1, dv1,
           tails, tailb, lgs, lgb, ld, docs, invc, spart, sblk, rq1, rq2, rk2, send, recv, load, hello):
    D = BLOCK
    L = X * BLOCK
    W2 = 2 * L
    R = D // Z
    me = lax.axis_index("seq")
    hd = lax.axis_index("head")
    z = me // X
    x = me % X
    scale = 1.0 / math.sqrt(D)
    half = X // 2

    def xdev(d):
        return (z * X + (x + d) % X, hd)

    def zdev(d):
        return (((z + d + Z) % Z) * X + x, hd)

    def pdev(i):
        return (z * X + (x + i // H) % X, (hd + i % H) % H)

    def each(blocks, work, carry=0):
        for b in blocks:
            carry = work(b, carry)
        return carry

    def put(src, dst, phase, dev):
        c = pltpu.make_async_remote_copy(
            src_ref=src, dst_ref=dst, send_sem=send.at[phase], recv_sem=recv.at[phase],
            device_id=dev, device_id_type=MESH)
        c.start()

    def got(ref, phase):
        pltpu.make_async_copy(ref, ref, recv.at[phase]).wait()

    def sent(ref, phase):
        pltpu.make_async_copy(ref, ref, send.at[phase]).wait()

    barrier = pltpu.get_barrier_semaphore()
    sources = (k1_in, v1_in, k2_in, q2_in, go_in, q1_in)
    near = [zdev(d) for d in NEAR[Z]] + [xdev(d) for d in range(1, X)]
    same_x = [(me, (hd + d) % H) for d in range(1, H)]
    for dev in near:
        pl.semaphore_signal(barrier, inc=1, device_id=dev, device_id_type=MESH)
    pltpu.make_async_copy(ld_in, ld, load.at[6]).start()
    for n, src in enumerate(sources):
        pltpu.make_async_copy(src, raw_in.at[n], load.at[n]).start()
    pltpu.make_async_copy(docs_in, docs, load.at[7]).start()
    for dev in same_x:
        pl.semaphore_signal(barrier, inc=1, device_id=dev, device_id_type=MESH)

    def greet(number, devices):
        for dev in devices:
            pl.semaphore_signal(hello.at[number], inc=1, device_id=dev, device_id_type=MESH)

    rows = lax.broadcasted_iota(jnp.int32, (D, D), 0)
    cols = lax.broadcasted_iota(jnp.int32, (D, D), 1)
    eye = rows == cols

    def to_row(col):
        return jnp.sum(jnp.where(eye, col, 0.0), axis=0, keepdims=True)

    def to_col(row):
        return jnp.sum(jnp.where(eye, row, 0.0), axis=1, keepdims=True)

    def heads_first(n):
        pltpu.make_async_copy(sources[n], raw_in.at[n], load.at[n]).wait()
        wide_in[n % 2] = raw_in[n].astype(F32)
        for h in range(X):
            hm[n, h] = wide_in[n % 2, :, h, :].astype(BF16)

    def exchange(src, dst, base, phase, apart=False):
        for d in AROUND[X]:
            put(src.at[(x + d) % X], dst.at[base + x], phase + (d - 1) * apart, xdev(d))
        dst[base + x] = src[x]

    pltpu.make_async_copy(ld_in, ld, load.at[6]).wait()
    heads_first(0)
    heads_first(1)
    for h in range(X):
        row = ld[h]
        col = jnp.sum(jnp.where(cols <= rows, row, 0.0), axis=1, keepdims=True)
        left = jnp.exp(jnp.sum(row, axis=1, keepdims=True) - col)
        spart[h] = dot_r(hm[0, h], hm[1, h].astype(F32) * left, TN).astype(BF16)
    pl.semaphore_wait(barrier, len(near) + len(same_x))
    greet(0, same_x)
    for number, reach in enumerate(FAR[Z]):
        if number == 0:
            greet(1, [zdev(reach), zdev(-reach)])

    exchange(ld, ldb, 0, LD)
    exchange(spart, sblk, 0, SP)
    heads_first(2)
    exchange(hm.at[2], kall, 2 * X, K2, True)
    heads_first(3)
    exchange(hm.at[3], qall, 0, Q2, True)
    for number, reach in enumerate(FAR[Z]):
        if number == 1:
            pl.semaphore_wait(hello.at[number], 2)
            greet(number + 1, [zdev(reach), zdev(-reach)])
    heads_first(4)
    exchange(hm.at[4], gall, 0, GO, True)
    exchange(hm.at[0], k1b, 0, K1)
    exchange(hm.at[1], v1b, 0, V1)
    heads_first(5)
    exchange(hm.at[5], q1b, 0, Q1)
    put(hm.at[2, x], kall.at[X + x], KA, zdev(1))
    put(hm.at[3, x], qall.at[X + x], QA, zdev(-1))
    put(hm.at[4, x], gall.at[X + x], GA, zdev(-1))
    pltpu.make_async_copy(docs_in, docs, load.at[7]).wait()
    pl.semaphore_wait(hello.at[0], len(same_x))

    got(ldb.at[pl.ds(0, X - 1)], LD)
    offset = jnp.zeros((1, 1), F32)
    ends = []
    for b in range(X):
        row = ldb[b]
        col = jnp.sum(jnp.where(cols <= rows, row, 0.0), axis=1, keepdims=True) + offset
        gcol[b] = col
        grow[b] = to_row(col)
        offset = offset + jnp.sum(row, axis=1, keepdims=True)
        ends.append(offset)
    g_end = offset
    arow[...] = jnp.broadcast_to(jnp.exp(g_end), (1, D))
    for b in range(X):
        tails[b] = jnp.exp(g_end - grow[b])

    got(sblk.at[pl.ds(0, X - 1)], SP)
    state = jnp.zeros((D, D), F32)
    for b in range(X):
        state = state + jnp.exp(g_end - ends[b]) * sblk[b].astype(F32)
    sst[...] = state.reshape(Z, R, D).astype(BF16)
    if FAR[Z]:
        pl.semaphore_wait(hello.at[len(FAR[Z])], 2)

    def far_first(i):
        return Z // 2 + ((i + 1) // 2) * (2 * (i % 2) - 1)

    def scan_send(src, dst, phase, decays=False):
        def one(i, c):
            d = far_first(i)
            to = (z + d) % Z
            if decays:
                put(arow, abuf.at[z], DEC, zdev(d))
            put(src.at[to], dst.at[z], phase, zdev(d))
            return c
        lax.fori_loop(0, Z - 1, one, 0)
        dst[z] = src[z]

    abuf[z] = arow[...]
    scan_send(sst, sbuf, SC1, True)

    def pass_on(ref, base, come, phase, dev):
        for d in AROUND[X]:
            at = (x - d + X) % X
            got(ref.at[pl.ds(0, 1)], come + d - 1)
            put(ref.at[base + at], ref.at[X + at], phase, dev)

    pass_on(kall, 2 * X, K2, KA, zdev(1))
    pass_on(qall, 0, Q2, QA, zdev(-1))
    pass_on(gall, 0, GO, GA, zdev(-1))

    for j in range(3 * X):
        for ref, first in ((kdoc, (z - 2) * X), (qdoc, z * X)):
            at = first + j
            inside = (at >= 0) & (at < Z * X)
            value = docs[jnp.clip(at, 0, Z * X - 1)]
            ref[j] = jnp.full((1, D), jnp.where(inside, value, -1), jnp.int32)

    got(kall.at[pl.ds(X, X)], KA)
    put(kall.at[pl.ds(X + 1, X - 1)], kall.at[pl.ds(1, X - 1)], KB, zdev(1))
    got(qall.at[pl.ds(X, X)], QA)
    put(qall.at[pl.ds(X, X - 1)], qall.at[pl.ds(2 * X, X - 1)], QB, zdev(-1))

    def scan_local(backward, pieces, results):
        m = jnp.zeros((R, D), F32)
        for i in range(Z):
            at = Z - 1 - i if backward else i
            results[at] = m.astype(BF16)
            m = abuf[at] * m + pieces[at].astype(F32)

    got(sbuf.at[pl.ds(0, Z - 1)], SC1)
    got(abuf.at[pl.ds(0, Z - 1)], DEC)
    scan_local(False, sbuf, mst)
    scan_send(mst, mbuf, SC2)
    got(gall.at[pl.ds(X, X)], GA)
    put(gall.at[pl.ds(X, X - 1)], gall.at[pl.ds(2 * X, X - 1)], GB, zdev(-1))

    wide = lax.broadcasted_iota(jnp.int32, (D, W2), 1)
    tall = lax.broadcasted_iota(jnp.int32, (D, W2), 0)

    def window(ref, first):
        return ref[pl.ds(first, 2 * X)].reshape(W2, D)

    def window_row(ref, first):
        return jnp.concatenate([ref[first + i] for i in range(2 * X)], axis=1)

    def probs(b, c):
        s = dot(qall[b], window(kall, b + 1), NT) * scale
        ok = (window_row(kdoc, b + 1) == docs[z * X + b]) & (wide <= tall + (W2 - D))
        s = jnp.where(ok, s, FLOOR)
        peak = jnp.max(s, axis=1, keepdims=True)
        mass = jnp.sum(jnp.where(ok, jnp.exp(s - peak), 0.0), axis=1, keepdims=True)
        lse = peak + jnp.log(mass)
        pf[b] = jnp.where(ok, jnp.exp(s - lse), 0.0)
        lser[b] = to_row(lse)
        return c

    probs(X - 1, 0)
    got(kall.at[pl.ds(1, X - 1)], KB)
    each(range(X - 1), probs)
    put(lser, lsall.at[pl.ds(X, X)], LA, zdev(-1))
    put(lser, lsall.at[pl.ds(2 * X, X)], LB, zdev(-2))
    lsall[pl.ds(0, X)] = lser[...]

    exchange(tails, tailb, 0, TL)
    got(k1b.at[pl.ds(0, X - 1)], K1)
    got(v1b.at[pl.ds(0, X - 1)], V1)
    got(q1b.at[pl.ds(0, X - 1)], Q1)
    g_row = jnp.concatenate([grow[b] for b in range(X)], axis=1)
    u_pos = lax.broadcasted_iota(jnp.int32, (D, L), 1)
    t_off = lax.broadcasted_iota(jnp.int32, (D, L), 0)
    k1all = k1b[...].reshape(L, D)
    v1all = v1b[...].reshape(L, D)

    def inner(b, c):
        low = u_pos <= t_off + b * D
        gap = gcol[b] - g_row
        w = jnp.where(low, jnp.exp(jnp.where(low, gap, 0.0)), 0.0)
        wts[b] = w
        a = dot(q1b[b], k1all, NT) * w
        aw[b] = a
        raw[b] = dot_l(a, v1all, NN)
        return c

    each(range(X), inner)

    def probs_t(b, c):
        s = dot(kall[2 * X + b], window(qall, b), NT) * scale
        ok = (window_row(qdoc, b) == docs[z * X + b]) & (wide >= tall)
        p = jnp.where(ok, jnp.exp(jnp.where(ok, s - window_row(lsall, b), 0.0)), 0.0)
        pt[b] = p
        gv[b] = dot(p.astype(BF16), window(gall, b), NN)
        return c

    got(lsall.at[pl.ds(X, X)], LA)
    probs_t(0, 0)
    got(qall.at[pl.ds(2 * X, X - 1)], QB)
    got(gall.at[pl.ds(2 * X, X - 1)], GB)
    got(lsall.at[pl.ds(2 * X, X)], LB)
    each(range(1, X), probs_t)

    got(mbuf.at[pl.ds(0, Z - 1)], SC2)
    m_state = mbuf[...].astype(F32).reshape(D, D).astype(BF16)

    def outer(b, c):
        r = raw[b] + jnp.exp(gcol[b]) * dot(q1b[b], m_state, NN)
        raw[b] = r
        pls[pl.ds(b, 1), :] = to_row(jnp.sum(r * r, axis=1, keepdims=True))
        pls[pl.ds(X + b, 1), :] = to_row(jnp.sum(r * gv[b], axis=1, keepdims=True))
        return c

    each(range(X), outer)

    def plane_send(i, c):
        put(pls, plb.at[i], PLN, pdev(i))
        return c

    lax.fori_loop(X * H // 2, X * H, plane_send, 0)
    lax.fori_loop(1, X * H // 2, plane_send, 0)
    plb[0] = pls[...]
    got(plb.at[pl.ds(1, X * H - 1)], PLN)
    sums = jnp.sum(plb[...], axis=0)
    inv_row = 1.0 / jnp.sqrt(sums[:X] / width_all + NORM_EPSILON)
    coef_row = inv_row * inv_row * inv_row * sums[X:] / width_all
    nrm[pl.ds(0, X), :] = inv_row
    nrm[pl.ds(X, X), :] = coef_row

    def finish(b, d_state):
        inv = to_col(nrm[pl.ds(b, 1), :])
        coef = to_col(nrm[pl.ds(X + b, 1), :])
        invc[b] = inv
        g = inv * gv[b] - raw[b] * coef
        rr[b] = g
        return d_state + dot(q1b[b], (g * jnp.exp(gcol[b])).astype(BF16), TN)

    d_state = each(range(X), finish, jnp.zeros((D, D), F32))
    sst2[...] = d_state.reshape(Z, R, D).astype(BF16)
    scan_send(sst2, sbuf2, SC3)
    for b in range(X):
        vall[2 * X + b] = (raw[b] * invc[b]).astype(BF16)
    put(vall.at[pl.ds(2 * X + half, half)], vall.at[pl.ds(X + half, half)], VA, zdev(1))
    put(vall.at[pl.ds(2 * X, half)], vall.at[pl.ds(X, half)], VB, zdev(1))

    def give_back(n, out, phase):
        for d in range(1, X):
            put(ost.at[n, (x + d) % X], out.at[x], phase, xdev(d))
        out[x] = ost[n, x]


    def inner_q(b, c):
        g = rr[b].astype(BF16)
        back = (dot(g, v1all, NT) * wts[b]).astype(BF16)
        bw[b] = back
        rlow[b] = g
        part = dot(back, k1all, NN) + jnp.exp(gcol[b]) * dot(g, m_state, NT)
        ost[0, b] = part.astype(BF16)
        return c

    each(range(X), inner_q)
    got(vall.at[pl.ds(X + half, half)], VA)
    put(vall.at[pl.ds(X + half, half)], vall.at[pl.ds(half, half)], VC, zdev(1))
    give_back(0, rq1, O0)
    q1all = q1b[...].reshape(L, D)
    rall = rlow[...].reshape(L, D)
    for b in range(X):
        own = pl.ds(b * D, D)
        ost[1, b] = dot(bw[:, :, own].reshape(L, D), q1all, TN).astype(BF16)
        ost[2, b] = dot(aw[:, :, own].reshape(L, D).astype(BF16), rall, TN).astype(BF16)
    got(vall.at[pl.ds(X, half)], VB)
    if half > 1:
        put(vall.at[pl.ds(X + 1, half - 1)], vall.at[pl.ds(1, half - 1)], VD, zdev(1))
    give_back(1, pk1, O1)
    give_back(2, pv1, O2)

    got(sbuf2.at[pl.ds(0, Z - 1)], SC3)
    scan_local(True, sbuf2, mst2)
    scan_send(mst2, mbuf2, SC4)

    def query_grads(b, c):
        p = pf[b]
        gp = dot(gall[b], window(vall, b + 1), NT)
        delta = jnp.sum(p.astype(BF16).astype(F32) * gp, axis=1, keepdims=True)
        delr[b] = to_row(delta)
        ds = (p * (gp - delta) * scale).astype(BF16)
        ost[3, b] = dot(ds, window(kall, b + 1), NN).astype(BF16)
        return c

    query_grads(X - 1, 0)
    got(vall.at[pl.ds(half, half)], VC)
    each(range(X - 2, half - 2, -1), query_grads)
    if half > 1:
        got(vall.at[pl.ds(1, half - 1)], VD)
        each(range(half - 2, -1, -1), query_grads)
    put(delr, dlall.at[pl.ds(X, X)], DA, zdev(-1))
    put(delr, dlall.at[pl.ds(2 * X, X)], DB, zdev(-2))
    dlall[pl.ds(0, X)] = delr[...]
    give_back(3, rq2, O3)

    got(dlall.at[pl.ds(X, X)], DA)
    got(dlall.at[pl.ds(2 * X, X)], DB)

    def key_grads(i, c):
        b = (x + i) % X
        gp = dot(vall[2 * X + b], window(gall, b), NT)
        ds = (pt[b] * (gp - window_row(dlall, b)) * scale).astype(BF16)
        part = dot(ds, window(qall, b), NN).astype(BF16)
        if i < X:
            ost[4, b] = part
        else:
            rk2[x] = part
        return c

    def key_send(i):
        put(ost.at[4, (x + i) % X], rk2.at[x], O4, xdev(i))

    key_grads(1, 0)

    got(mbuf2.at[pl.ds(0, Z - 1)], SC4)
    lgs[...] = mbuf2[...].astype(F32).reshape(D, D).astype(BF16)
    for d in FARTHEST[X]:
        put(lgs, lgb.at[x], LG, xdev(d))
    key_send(1)
    lgb[x] = lgs[...]
    for i in range(2, X):
        key_grads(i, 0)
        key_send(i)
    key_grads(X, 0)

    got(pk1.at[pl.ds(0, X - 1)], O1)
    got(pv1.at[pl.ds(0, X - 1)], O2)
    got(tailb.at[pl.ds(0, X - 1)], TL)

    def result(out, held, phase):
        got(held.at[pl.ds(0, X - 1)], phase)
        for h in range(X):
            out[:, h, :] = held[h].astype(F32)

    result(o_q1, rq1, O0)
    result(o_q2, rq2, O3)
    got(lgb.at[pl.ds(0, X - 1)], LG)

    def state_grads(h, c):
        tail = to_col(tailb[h])
        later = lgb[h]
        o_k1[:, h, :] = pk1[h].astype(F32) + tail * dot(hm[1, h], later, NT)
        o_v1[:, h, :] = pv1[h].astype(F32) + tail * dot(hm[0, h], later, NN)
        return c

    each(range(X), state_grads)

    result(o_k2, rk2, O4)
    for ref, phase in ((ldb, LD), (k1b, K1), (v1b, V1), (q1b, Q1),
                       (tailb, TL), (rq1, O0), (pk1, O1), (pv1, O2), (rq2, O3), (rk2, O4), (lgb, LG), (sblk, SP)):
        sent(ref.at[pl.ds(0, X - 1)], phase)
    for phase in (K2, Q2, GO):
        for d in range(1, X):
            sent(kall.at[pl.ds(0, 1)], phase + d - 1)
    for ref, phase in ((sbuf, SC1), (abuf, DEC), (mbuf, SC2), (sbuf2, SC3), (mbuf2, SC4)):
        sent(ref.at[pl.ds(0, Z - 1)], phase)
    for ref, phase in ((kall, KA), (qall, QA), (gall, GA), (lser, LA), (lser, LB), (delr, DA), (delr, DB)):
        sent(ref.at[pl.ds(0, X)], phase)
    for ref, phase in ((kall, KB), (qall, QB), (gall, GB)):
        sent(ref.at[pl.ds(0, X - 1)], phase)
    for phase in (VA, VB, VC):
        sent(vall.at[pl.ds(0, half)], phase)
    if half > 1:
        sent(vall.at[pl.ds(0, half - 1)], VD)
    sent(plb.at[pl.ds(1, X * H - 1)], PLN)


def place(*refs):
    ins, outs, store = refs[:5], refs[5:10], refs[10]
    for n in range(5):
        pltpu.make_async_copy(ins[n], outs[n], store.at[n]).start()
    for n in range(5):
        pltpu.make_async_copy(ins[n], outs[n], store.at[n]).wait()


def make_body(Z, X, H):
    D = BLOCK

    def vm(*shape, dtype=F32):
        return pltpu.VMEM(shape, dtype)

    def body(q1, k1, v1, ld, q2, k2, go, docs):
        L = X * D
        results = [jax.ShapeDtypeStruct((D, X, D), F32)] * 5
        low = functools.partial(vm, dtype=BF16)
        scratch = [
            low(6, D, X, D), vm(2, D, X, D), low(6, X, D, D),
            low(X, D, D), low(X, D, D), low(X, D, D),
            low(3 * X, D, D), low(3 * X, D, D), low(3 * X, D, D), low(3 * X, D, D),
            vm(X, 1, D), vm(X, D, 1), vm(X, 1, D),
            vm(X, D, L), vm(X, D, L), vm(X, D, 2 * L), vm(X, D, 2 * L),
            vm(X, 1, D), vm(X, 1, D), vm(3 * X, 1, D), vm(3 * X, 1, D),
            vm(3 * X, 1, D, dtype=jnp.int32), vm(3 * X, 1, D, dtype=jnp.int32),
            low(Z, D // Z, D), low(Z, D // Z, D), low(Z, D // Z, D), low(Z, D // Z, D),
            low(Z, D // Z, D), low(Z, D // Z, D), low(Z, D // Z, D), low(Z, D // Z, D),
            vm(Z, 1, D), vm(1, D),
            vm(X, D, D), vm(X, D, D), vm(X, D, D),
            vm(2 * X, D), vm(X * H, 2 * X, D), vm(2 * X, D),
            low(5, X, D, D), low(X, D, D), low(X, D, D),
            low(X, D, L), low(X, D, D), vm(X, D, D), vm(X, D, D),
            vm(X, 1, D), vm(X, 1, D), low(D, D), low(X, D, D),
            vm(X, 1, D), pltpu.SMEM((Z * X,), jnp.int32), vm(X, D, 1),
            low(X, D, D), low(X, D, D), low(X, D, D), low(X, D, D), low(X, D, D),
            pltpu.SemaphoreType.DMA((NSEM,)), pltpu.SemaphoreType.DMA((NSEM,)),
            pltpu.SemaphoreType.DMA((8,)), pltpu.SemaphoreType.REGULAR((NHELLO,)),
        ]
        vmem = pl.BlockSpec(memory_space=pltpu.VMEM)
        hbm = pl.BlockSpec(memory_space=pltpu.HBM)
        outs = pl.pallas_call(
            functools.partial(kernel, Z, X, H, float(X * H * D)),
            out_shape=results,
            in_specs=[hbm] * 8,
            out_specs=[vmem] * 5,
            scratch_shapes=scratch,
            compiler_params=pltpu.CompilerParams(
                collective_id=0, has_side_effects=True, vmem_limit_bytes=20 * 1024 * 1024),
        )(*[pltpu.with_memory_space_constraint(a, pltpu.HBM)
            for a in (q1, k1, v1, q2, k2, go, ld.reshape(X, 1, D), docs)])
        return tuple(pl.pallas_call(
            place,
            out_shape=results,
            in_specs=[vmem] * 5,
            out_specs=[hbm] * 5,
            scratch_shapes=[pltpu.SemaphoreType.DMA((5,))],
            compiler_params=pltpu.CompilerParams(vmem_limit_bytes=8 * 1024 * 1024),
        )(*outs))

    return body


def solution(mesh):
    split_both = P("seq", "head", None)
    placed = (split_both,) * 3 + (P("head", "seq"),) + (split_both,) * 3 + (P(),)
    return jax.shard_map(
        make_body(mesh.shape["seq"] // ROW, ROW, mesh.shape["head"]),
        mesh=mesh,
        in_specs=placed,
        out_specs=(split_both,) * 5,
        check_vma=False,
    )
```

```python
import functools
import math

import jax
import jax.numpy as jnp
from jax import lax
from jax.experimental import pallas as pl
from jax.experimental.pallas import tpu as pltpu
from jax.sharding import PartitionSpec as P

BLOCK = 128
ROW = 4
NORM_EPSILON = 1e-05
FLOOR = -1e30
MESH = pl.DeviceIdType.MESH
F32 = jnp.float32
BF16 = jnp.bfloat16

(LD, K1, V1, Q1, TL, SC1, DEC, SC2, KA, KB, QA, QB, GA, GB, LA, LB, PLN,
 SC3, SC4, VA, VB, VC, VD, DA, DB, O0, O1, O2, O3, O4, LG, SP) = range(32)
K2, Q2, GO = 32, 35, 38
NSEM = 41
NHELLO = 3
NEAR = {16: (1, -1, 2, -2), 4: (1, -1, 2)}
AROUND = {4: (1, 3, 2), 2: (1,)}
FARTHEST = {4: (2, 1, 3), 2: (1,)}
FAR = {16: (2, 4), 4: ()}

NN = (((1,), (0,)), ((), ()))
NT = (((1,), (1,)), ((), ()))
TN = (((0,), (0,)), ((), ()))


def dot(a, b, dims):
    return lax.dot_general(a, b, dims, preferred_element_type=F32)


def split(a):
    high = a.astype(BF16)
    return high, (a - high.astype(F32)).astype(BF16)


def dot_l(a, b, dims):
    high, low = split(a)
    return dot(high, b, dims) + dot(low, b, dims)


def dot_r(a, b, dims):
    high, low = split(b)
    return dot(a, high, dims) + dot(a, low, dims)


def kernel(Z, X, H, width_all, q1_in, k1_in, v1_in, q2_in, k2_in, go_in, ld_in, docs_in,
           o_q1, o_k1, o_v1, o_q2, o_k2,
           raw_in, wide_in, hm, q1b, k1b, v1b, kall, qall, gall, vall, ldb, gcol, grow,
           wts, aw, pf, pt, lser, delr, lsall, dlall, kdoc, qdoc,
           sst, sbuf, mst, mbuf, sst2, sbuf2, mst2, mbuf2, abuf, arow,
           raw, gv, rr, pls, plb, nrm, ost, pk1, pv1, bw, rlow, dk1, dv1,
           tails, tailb, lgs, lgb, ld, docs, invc, spart, sblk, rq1, rq2, rk2, send, recv, load, hello):
    D = BLOCK
    L = X * BLOCK
    W2 = 2 * L
    R = D // Z
    me = lax.axis_index("seq")
    hd = lax.axis_index("head")
    z = me // X
    x = me % X
    scale = 1.0 / math.sqrt(D)
    half = X // 2

    def xdev(d):
        return (z * X + (x + d) % X, hd)

    def zdev(d):
        return (((z + d + Z) % Z) * X + x, hd)

    def pdev(i):
        return (z * X + (x + i // H) % X, (hd + i % H) % H)

    def each(blocks, work, carry=0):
        for b in blocks:
            carry = work(b, carry)
        return carry

    def put(src, dst, phase, dev):
        c = pltpu.make_async_remote_copy(
            src_ref=src, dst_ref=dst, send_sem=send.at[phase], recv_sem=recv.at[phase],
            device_id=dev, device_id_type=MESH)
        c.start()

    def got(ref, phase):
        pltpu.make_async_copy(ref, ref, recv.at[phase]).wait()

    def sent(ref, phase):
        pltpu.make_async_copy(ref, ref, send.at[phase]).wait()

    barrier = pltpu.get_barrier_semaphore()
    sources = (k1_in, v1_in, k2_in, q2_in, go_in, q1_in)
    near = [zdev(d) for d in NEAR[Z]] + [xdev(d) for d in range(1, X)]
    same_x = [(me, (hd + d) % H) for d in range(1, H)]
    for dev in near:
        pl.semaphore_signal(barrier, inc=1, device_id=dev, device_id_type=MESH)
    pltpu.make_async_copy(ld_in, ld, load.at[6]).start()
    for n, src in enumerate(sources):
        pltpu.make_async_copy(src, raw_in.at[n], load.at[n]).start()
    pltpu.make_async_copy(docs_in, docs, load.at[7]).start()
    for dev in same_x:
        pl.semaphore_signal(barrier, inc=1, device_id=dev, device_id_type=MESH)

    def greet(number, devices):
        for dev in devices:
            pl.semaphore_signal(hello.at[number], inc=1, device_id=dev, device_id_type=MESH)

    rows = lax.broadcasted_iota(jnp.int32, (D, D), 0)
    cols = lax.broadcasted_iota(jnp.int32, (D, D), 1)
    eye = rows == cols

    def to_row(col):
        return jnp.sum(jnp.where(eye, col, 0.0), axis=0, keepdims=True)

    def to_col(row):
        return jnp.sum(jnp.where(eye, row, 0.0), axis=1, keepdims=True)

    def heads_first(n):
        pltpu.make_async_copy(sources[n], raw_in.at[n], load.at[n]).wait()
        wide_in[n % 2] = raw_in[n].astype(F32)
        for h in range(X):
            hm[n, h] = wide_in[n % 2, :, h, :].astype(BF16)

    def exchange(src, dst, base, phase, apart=False):
        for d in (AROUND if apart else FARTHEST)[X]:
            put(src.at[(x + d) % X], dst.at[base + x], phase + (d - 1) * apart, xdev(d))
        dst[base + x] = src[x]

    pltpu.make_async_copy(ld_in, ld, load.at[6]).wait()
    heads_first(0)
    heads_first(1)
    for h in range(X):
        row = ld[h]
        col = jnp.sum(jnp.where(cols <= rows, row, 0.0), axis=1, keepdims=True)
        left = jnp.exp(jnp.sum(row, axis=1, keepdims=True) - col)
        spart[h] = dot_r(hm[0, h], hm[1, h].astype(F32) * left, TN).astype(BF16)
    pl.semaphore_wait(barrier, len(near) + len(same_x))
    greet(0, same_x)
    for number, reach in enumerate(FAR[Z]):
        if number == 0:
            greet(1, [zdev(reach), zdev(-reach)])

    exchange(ld, ldb, 0, LD)
    exchange(spart, sblk, 0, SP)
    heads_first(2)
    exchange(hm.at[2], kall, 2 * X, K2, True)
    heads_first(3)
    exchange(hm.at[3], qall, 0, Q2, True)
    for number, reach in enumerate(FAR[Z]):
        if number == 1:
            pl.semaphore_wait(hello.at[number], 2)
            greet(number + 1, [zdev(reach), zdev(-reach)])
    heads_first(4)
    exchange(hm.at[4], gall, 0, GO, True)
    exchange(hm.at[0], k1b, 0, K1)
    exchange(hm.at[1], v1b, 0, V1)
    heads_first(5)
    exchange(hm.at[5], q1b, 0, Q1)
    put(hm.at[2, x], kall.at[X + x], KA, zdev(1))
    put(hm.at[3, x], qall.at[X + x], QA, zdev(-1))
    put(hm.at[4, x], gall.at[X + x], GA, zdev(-1))
    pltpu.make_async_copy(docs_in, docs, load.at[7]).wait()
    pl.semaphore_wait(hello.at[0], len(same_x))

    got(ldb.at[pl.ds(0, X - 1)], LD)
    offset = jnp.zeros((1, 1), F32)
    ends = []
    for b in range(X):
        row = ldb[b]
        col = jnp.sum(jnp.where(cols <= rows, row, 0.0), axis=1, keepdims=True) + offset
        gcol[b] = col
        grow[b] = to_row(col)
        offset = offset + jnp.sum(row, axis=1, keepdims=True)
        ends.append(offset)
    g_end = offset
    arow[...] = jnp.broadcast_to(jnp.exp(g_end), (1, D))
    for b in range(X):
        tails[b] = jnp.exp(g_end - grow[b])

    got(sblk.at[pl.ds(0, X - 1)], SP)
    state = jnp.zeros((D, D), F32)
    for b in range(X):
        state = state + jnp.exp(g_end - ends[b]) * sblk[b].astype(F32)
    sst[...] = state.reshape(Z, R, D).astype(BF16)
    if FAR[Z]:
        pl.semaphore_wait(hello.at[len(FAR[Z])], 2)

    def far_first(i):
        return Z // 2 + ((i + 1) // 2) * (2 * (i % 2) - 1)

    def scan_send(src, dst, phase, decays=False):
        def one(i, c):
            d = far_first(i)
            to = (z + d) % Z
            if decays:
                put(arow, abuf.at[z], DEC, zdev(d))
            put(src.at[to], dst.at[z], phase, zdev(d))
            return c
        lax.fori_loop(0, Z - 1, one, 0)
        dst[z] = src[z]

    abuf[z] = arow[...]
    scan_send(sst, sbuf, SC1, True)

    def pass_on(ref, base, come, phase, dev):
        for d in AROUND[X]:
            at = (x - d + X) % X
            got(ref.at[pl.ds(0, 1)], come + d - 1)
            put(ref.at[base + at], ref.at[X + at], phase, dev)

    pass_on(kall, 2 * X, K2, KA, zdev(1))
    pass_on(qall, 0, Q2, QA, zdev(-1))
    pass_on(gall, 0, GO, GA, zdev(-1))

    for j in range(3 * X):
        for ref, first in ((kdoc, (z - 2) * X), (qdoc, z * X)):
            at = first + j
            inside = (at >= 0) & (at < Z * X)
            value = docs[jnp.clip(at, 0, Z * X - 1)]
            ref[j] = jnp.full((1, D), jnp.where(inside, value, -1), jnp.int32)

    got(kall.at[pl.ds(X, X)], KA)
    put(kall.at[pl.ds(X + 1, X - 1)], kall.at[pl.ds(1, X - 1)], KB, zdev(1))
    got(qall.at[pl.ds(X, X)], QA)
    put(qall.at[pl.ds(X, X - 1)], qall.at[pl.ds(2 * X, X - 1)], QB, zdev(-1))

    def scan_local(backward, pieces, results):
        m = jnp.zeros((R, D), F32)
        for i in range(Z):
            at = Z - 1 - i if backward else i
            results[at] = m.astype(BF16)
            m = abuf[at] * m + pieces[at].astype(F32)

    got(sbuf.at[pl.ds(0, Z - 1)], SC1)
    got(abuf.at[pl.ds(0, Z - 1)], DEC)
    scan_local(False, sbuf, mst)
    scan_send(mst, mbuf, SC2)
    got(gall.at[pl.ds(X, X)], GA)
    put(gall.at[pl.ds(X, X - 1)], gall.at[pl.ds(2 * X, X - 1)], GB, zdev(-1))

    wide = lax.broadcasted_iota(jnp.int32, (D, W2), 1)
    tall = lax.broadcasted_iota(jnp.int32, (D, W2), 0)

    def window(ref, first):
        return ref[pl.ds(first, 2 * X)].reshape(W2, D)

    def window_row(ref, first):
        return jnp.concatenate([ref[first + i] for i in range(2 * X)], axis=1)

    def probs(b, c):
        s = dot(qall[b], window(kall, b + 1), NT) * scale
        ok = (window_row(kdoc, b + 1) == docs[z * X + b]) & (wide <= tall + (W2 - D))
        s = jnp.where(ok, s, FLOOR)
        peak = jnp.max(s, axis=1, keepdims=True)
        mass = jnp.sum(jnp.where(ok, jnp.exp(s - peak), 0.0), axis=1, keepdims=True)
        lse = peak + jnp.log(mass)
        pf[b] = jnp.where(ok, jnp.exp(s - lse), 0.0)
        lser[b] = to_row(lse)
        return c

    probs(X - 1, 0)
    got(kall.at[pl.ds(1, X - 1)], KB)
    each(range(X - 1), probs)
    put(lser, lsall.at[pl.ds(X, X)], LA, zdev(-1))
    put(lser, lsall.at[pl.ds(2 * X, X)], LB, zdev(-2))
    lsall[pl.ds(0, X)] = lser[...]

    exchange(tails, tailb, 0, TL)
    got(k1b.at[pl.ds(0, X - 1)], K1)
    got(v1b.at[pl.ds(0, X - 1)], V1)
    got(q1b.at[pl.ds(0, X - 1)], Q1)
    g_row = jnp.concatenate([grow[b] for b in range(X)], axis=1)
    u_pos = lax.broadcasted_iota(jnp.int32, (D, L), 1)
    t_off = lax.broadcasted_iota(jnp.int32, (D, L), 0)
    k1all = k1b[...].reshape(L, D)
    v1all = v1b[...].reshape(L, D)

    def inner(b, c):
        low = u_pos <= t_off + b * D
        gap = gcol[b] - g_row
        w = jnp.where(low, jnp.exp(jnp.where(low, gap, 0.0)), 0.0)
        wts[b] = w
        a = dot(q1b[b], k1all, NT) * w
        aw[b] = a
        raw[b] = dot_l(a, v1all, NN)
        return c

    each(range(X), inner)

    def probs_t(b, c):
        s = dot(kall[2 * X + b], window(qall, b), NT) * scale
        ok = (window_row(qdoc, b) == docs[z * X + b]) & (wide >= tall)
        p = jnp.where(ok, jnp.exp(jnp.where(ok, s - window_row(lsall, b), 0.0)), 0.0)
        pt[b] = p
        gv[b] = dot(p.astype(BF16), window(gall, b), NN)
        return c

    got(lsall.at[pl.ds(X, X)], LA)
    probs_t(0, 0)
    got(qall.at[pl.ds(2 * X, X - 1)], QB)
    got(gall.at[pl.ds(2 * X, X - 1)], GB)
    got(lsall.at[pl.ds(2 * X, X)], LB)
    each(range(1, X), probs_t)

    got(mbuf.at[pl.ds(0, Z - 1)], SC2)
    m_state = mbuf[...].astype(F32).reshape(D, D).astype(BF16)

    def outer(b, c):
        r = raw[b] + jnp.exp(gcol[b]) * dot(q1b[b], m_state, NN)
        raw[b] = r
        pls[pl.ds(b, 1), :] = to_row(jnp.sum(r * r, axis=1, keepdims=True))
        pls[pl.ds(X + b, 1), :] = to_row(jnp.sum(r * gv[b], axis=1, keepdims=True))
        return c

    each(range(X), outer)

    def plane_send(i, c):
        put(pls, plb.at[i], PLN, pdev(i))
        return c

    lax.fori_loop(X * H // 2, X * H, plane_send, 0)
    lax.fori_loop(1, X * H // 2, plane_send, 0)
    plb[0] = pls[...]
    got(plb.at[pl.ds(1, X * H - 1)], PLN)
    sums = jnp.sum(plb[...], axis=0)
    inv_row = 1.0 / jnp.sqrt(sums[:X] / width_all + NORM_EPSILON)
    coef_row = inv_row * inv_row * inv_row * sums[X:] / width_all
    nrm[pl.ds(0, X), :] = inv_row
    nrm[pl.ds(X, X), :] = coef_row

    def finish(b, d_state):
        inv = to_col(nrm[pl.ds(b, 1), :])
        coef = to_col(nrm[pl.ds(X + b, 1), :])
        invc[b] = inv
        g = inv * gv[b] - raw[b] * coef
        rr[b] = g
        return d_state + dot(q1b[b], (g * jnp.exp(gcol[b])).astype(BF16), TN)

    d_state = each(range(X), finish, jnp.zeros((D, D), F32))
    sst2[...] = d_state.reshape(Z, R, D).astype(BF16)
    scan_send(sst2, sbuf2, SC3)
    for b in range(X):
        vall[2 * X + b] = (raw[b] * invc[b]).astype(BF16)
    put(vall.at[pl.ds(2 * X + half, half)], vall.at[pl.ds(X + half, half)], VA, zdev(1))
    put(vall.at[pl.ds(2 * X, half)], vall.at[pl.ds(X, half)], VB, zdev(1))

    def give_back(n, out, phase):
        for d in FARTHEST[X]:
            put(ost.at[n, (x + d) % X], out.at[x], phase, xdev(d))
        out[x] = ost[n, x]


    def inner_q(b, c):
        g = rr[b].astype(BF16)
        back = (dot(g, v1all, NT) * wts[b]).astype(BF16)
        bw[b] = back
        rlow[b] = g
        part = dot(back, k1all, NN) + jnp.exp(gcol[b]) * dot(g, m_state, NT)
        ost[0, b] = part.astype(BF16)
        return c

    each(range(X), inner_q)
    got(vall.at[pl.ds(X + half, half)], VA)
    put(vall.at[pl.ds(X + half, half)], vall.at[pl.ds(half, half)], VC, zdev(1))
    give_back(0, rq1, O0)
    q1all = q1b[...].reshape(L, D)
    rall = rlow[...].reshape(L, D)
    for b in range(X):
        own = pl.ds(b * D, D)
        ost[1, b] = dot(bw[:, :, own].reshape(L, D), q1all, TN).astype(BF16)
        ost[2, b] = dot(aw[:, :, own].reshape(L, D).astype(BF16), rall, TN).astype(BF16)
    got(vall.at[pl.ds(X, half)], VB)
    if half > 1:
        put(vall.at[pl.ds(X + 1, half - 1)], vall.at[pl.ds(1, half - 1)], VD, zdev(1))
    give_back(1, pk1, O1)
    give_back(2, pv1, O2)

    got(sbuf2.at[pl.ds(0, Z - 1)], SC3)
    scan_local(True, sbuf2, mst2)
    scan_send(mst2, mbuf2, SC4)

    def query_grads(b, c):
        p = pf[b]
        gp = dot(gall[b], window(vall, b + 1), NT)
        delta = jnp.sum(p.astype(BF16).astype(F32) * gp, axis=1, keepdims=True)
        delr[b] = to_row(delta)
        ds = (p * (gp - delta) * scale).astype(BF16)
        ost[3, b] = dot(ds, window(kall, b + 1), NN).astype(BF16)
        return c

    query_grads(X - 1, 0)
    got(vall.at[pl.ds(half, half)], VC)
    each(range(X - 2, half - 2, -1), query_grads)
    if half > 1:
        got(vall.at[pl.ds(1, half - 1)], VD)
        each(range(half - 2, -1, -1), query_grads)
    put(delr, dlall.at[pl.ds(X, X)], DA, zdev(-1))
    put(delr, dlall.at[pl.ds(2 * X, X)], DB, zdev(-2))
    dlall[pl.ds(0, X)] = delr[...]
    give_back(3, rq2, O3)

    got(dlall.at[pl.ds(X, X)], DA)
    got(dlall.at[pl.ds(2 * X, X)], DB)

    def key_grads(i, c):
        b = (x + i) % X
        gp = dot(vall[2 * X + b], window(gall, b), NT)
        ds = (pt[b] * (gp - window_row(dlall, b)) * scale).astype(BF16)
        part = dot(ds, window(qall, b), NN).astype(BF16)
        if i < X:
            ost[4, b] = part
        else:
            rk2[x] = part
        return c

    def key_send(i):
        put(ost.at[4, (x + i) % X], rk2.at[x], O4, xdev(i))

    order = FARTHEST[X]
    key_grads(order[0], 0)

    got(mbuf2.at[pl.ds(0, Z - 1)], SC4)
    lgs[...] = mbuf2[...].astype(F32).reshape(D, D).astype(BF16)
    for d in FARTHEST[X]:
        put(lgs, lgb.at[x], LG, xdev(d))
    key_send(order[0])
    lgb[x] = lgs[...]
    for i in order[1:]:
        key_grads(i, 0)
        key_send(i)
    key_grads(X, 0)

    got(pk1.at[pl.ds(0, X - 1)], O1)
    got(pv1.at[pl.ds(0, X - 1)], O2)
    got(tailb.at[pl.ds(0, X - 1)], TL)

    def result(out, held, phase):
        got(held.at[pl.ds(0, X - 1)], phase)
        for h in range(X):
            out[:, h, :] = held[h].astype(F32)

    result(o_q1, rq1, O0)
    result(o_q2, rq2, O3)
    got(lgb.at[pl.ds(0, X - 1)], LG)

    def state_grads(h, c):
        tail = to_col(tailb[h])
        later = lgb[h]
        o_k1[:, h, :] = pk1[h].astype(F32) + tail * dot(hm[1, h], later, NT)
        o_v1[:, h, :] = pv1[h].astype(F32) + tail * dot(hm[0, h], later, NN)
        return c

    each(range(X), state_grads)

    result(o_k2, rk2, O4)
    for ref, phase in ((ldb, LD), (k1b, K1), (v1b, V1), (q1b, Q1),
                       (tailb, TL), (rq1, O0), (pk1, O1), (pv1, O2), (rq2, O3), (rk2, O4), (lgb, LG), (sblk, SP)):
        sent(ref.at[pl.ds(0, X - 1)], phase)
    for phase in (K2, Q2, GO):
        for d in range(1, X):
            sent(kall.at[pl.ds(0, 1)], phase + d - 1)
    for ref, phase in ((sbuf, SC1), (abuf, DEC), (mbuf, SC2), (sbuf2, SC3), (mbuf2, SC4)):
        sent(ref.at[pl.ds(0, Z - 1)], phase)
    for ref, phase in ((kall, KA), (qall, QA), (gall, GA), (lser, LA), (lser, LB), (delr, DA), (delr, DB)):
        sent(ref.at[pl.ds(0, X)], phase)
    for ref, phase in ((kall, KB), (qall, QB), (gall, GB)):
        sent(ref.at[pl.ds(0, X - 1)], phase)
    for phase in (VA, VB, VC):
        sent(vall.at[pl.ds(0, half)], phase)
    if half > 1:
        sent(vall.at[pl.ds(0, half - 1)], VD)
    sent(plb.at[pl.ds(1, X * H - 1)], PLN)


def place(*refs):
    ins, outs, store = refs[:5], refs[5:10], refs[10]
    for n in range(5):
        pltpu.make_async_copy(ins[n], outs[n], store.at[n]).start()
    for n in range(5):
        pltpu.make_async_copy(ins[n], outs[n], store.at[n]).wait()


def make_body(Z, X, H):
    D = BLOCK

    def vm(*shape, dtype=F32):
        return pltpu.VMEM(shape, dtype)

    def body(q1, k1, v1, ld, q2, k2, go, docs):
        L = X * D
        results = [jax.ShapeDtypeStruct((D, X, D), F32)] * 5
        low = functools.partial(vm, dtype=BF16)
        scratch = [
            low(6, D, X, D), vm(2, D, X, D), low(6, X, D, D),
            low(X, D, D), low(X, D, D), low(X, D, D),
            low(3 * X, D, D), low(3 * X, D, D), low(3 * X, D, D), low(3 * X, D, D),
            vm(X, 1, D), vm(X, D, 1), vm(X, 1, D),
            vm(X, D, L), vm(X, D, L), vm(X, D, 2 * L), vm(X, D, 2 * L),
            vm(X, 1, D), vm(X, 1, D), vm(3 * X, 1, D), vm(3 * X, 1, D),
            vm(3 * X, 1, D, dtype=jnp.int32), vm(3 * X, 1, D, dtype=jnp.int32),
            low(Z, D // Z, D), low(Z, D // Z, D), low(Z, D // Z, D), low(Z, D // Z, D),
            low(Z, D // Z, D), low(Z, D // Z, D), low(Z, D // Z, D), low(Z, D // Z, D),
            vm(Z, 1, D), vm(1, D),
            vm(X, D, D), vm(X, D, D), vm(X, D, D),
            vm(2 * X, D), vm(X * H, 2 * X, D), vm(2 * X, D),
            low(5, X, D, D), low(X, D, D), low(X, D, D),
            low(X, D, L), low(X, D, D), vm(X, D, D), vm(X, D, D),
            vm(X, 1, D), vm(X, 1, D), low(D, D), low(X, D, D),
            vm(X, 1, D), pltpu.SMEM((Z * X,), jnp.int32), vm(X, D, 1),
            low(X, D, D), low(X, D, D), low(X, D, D), low(X, D, D), low(X, D, D),
            pltpu.SemaphoreType.DMA((NSEM,)), pltpu.SemaphoreType.DMA((NSEM,)),
            pltpu.SemaphoreType.DMA((8,)), pltpu.SemaphoreType.REGULAR((NHELLO,)),
        ]
        vmem = pl.BlockSpec(memory_space=pltpu.VMEM)
        hbm = pl.BlockSpec(memory_space=pltpu.HBM)
        outs = pl.pallas_call(
            functools.partial(kernel, Z, X, H, float(X * H * D)),
            out_shape=results,
            in_specs=[hbm] * 8,
            out_specs=[vmem] * 5,
            scratch_shapes=scratch,
            compiler_params=pltpu.CompilerParams(
                collective_id=0, has_side_effects=True, vmem_limit_bytes=20 * 1024 * 1024),
        )(*[pltpu.with_memory_space_constraint(a, pltpu.HBM)
            for a in (q1, k1, v1, q2, k2, go, ld.reshape(X, 1, D), docs)])
        return tuple(pl.pallas_call(
            place,
            out_shape=results,
            in_specs=[vmem] * 5,
            out_specs=[hbm] * 5,
            scratch_shapes=[pltpu.SemaphoreType.DMA((5,))],
            compiler_params=pltpu.CompilerParams(vmem_limit_bytes=8 * 1024 * 1024),
        )(*outs))

    return body


def solution(mesh):
    split_both = P("seq", "head", None)
    placed = (split_both,) * 3 + (P("head", "seq"),) + (split_both,) * 3 + (P(),)
    return jax.shard_map(
        make_body(mesh.shape["seq"] // ROW, ROW, mesh.shape["head"]),
        mesh=mesh,
        in_specs=placed,
        out_specs=(split_both,) * 5,
        check_vma=False,
    )
```
